256 devices in a mesh: grp: 4 (over z_hi), gx: 16 (over z_lo, y, core), gy: 4 (over x).
Axes of the slice: x: 4, y: 4, z: 8 (z_hi: 4, z_lo: 2; z = z_hi * 2 + z_lo), core: 2. Of those that a mesh axis runs over, the one named last changes fastest.
Arguments:
- populations: float32 [27, 64, 32, 512], P(None, 'gx', 'gy', 'grp'), may hold values from 0 to 1, as said below
- thermal: float32 [7, 64, 32, 512], P(None, ('gx', 'grp'), 'gy'), may hold values from 0 to 1, as said below
- velocity_prev: float32 [3, 64, 32, 512], P(None, 'gx', 'gy', 'grp'), may hold values from -0.3 to 0.3
- solid: int32 [64, 32, 512], P('gx', 'gy', 'grp'), may hold values 0 or 1
- phase_ids: int32 [64, 32, 512], P(('gx', 'grp'), 'gy'), may hold values from 0 to 3
- conductivity: float32 [4], replicated, may hold values from 0.02 to 0.3
- rates: float32 [27], replicated, may hold values from 0.7 to 1.7
Outputs:
- populations_out: float32 [27, 64, 32, 512], P(None, 'gx', 'gy', 'grp')
- thermal_out: float32 [7, 64, 32, 512], P(None, ('gx', 'grp'), 'gy')
The draws below stay inside these ranges and needn't reach their ends.
Inputs may be any that keep to these rules, and one draw needn't show every extreme that they name: `populations`: positive. `thermal`: positive.
All inputs are finite; a program needn't handle non-finite values. No bound on the sum of `solid` on one device may be relied on, other than what follows from the above.
Results may differ from the reference program's by a relative error of at most 0.0001.
Values sent between devices are 32-bit elements; how exact they have to be, the bound alone decides.
A program may use at most 64 MiB of HBM per device.

```python
import math
import jax
import jax.numpy as jnp
import numpy as np
from jax import lax

STEPS = 4
WINDOWS = 2
PHASES = 4
NX = 64
NY = 32
NZ = 512


OFFSET_TABLE = [(number // 9 - 1, number // 3 % 3 - 1, number % 3 - 1) for number in range(27)]


LATTICE_WEIGHTS = np.array([np.prod([2.0 / 3.0 if component == 0 else 1.0 / 6.0 for component in triple]) for triple in OFFSET_TABLE])


HEAT_WEIGHTS = np.array([0.25] + [0.125] * 6)


def draw_populations(key, part):
    weights = jnp.asarray(LATTICE_WEIGHTS, jnp.float32)
    noise = jax.random.normal(jax.random.fold_in(key, 12), (27, NX, NY, NZ), jnp.float32)
    factor = jnp.exp(0.25 * jnp.clip(noise, -3.0, 3.0))
    return weights[:, None, None, None] * factor


def draw_thermal(key, part):
    weights = jnp.asarray(HEAT_WEIGHTS, jnp.float32)
    level = jax.random.uniform(jax.random.fold_in(key, 23), (NX, NY, NZ), jnp.float32, 0.5, 1.5)
    noise = jax.random.normal(jax.random.fold_in(key, 24), (7, NX, NY, NZ), jnp.float32)
    factor = jnp.exp(0.2 * jnp.clip(noise, -3.0, 3.0))
    return weights[:, None, None, None] * level[None] * factor


def touch_ends(values, key, least, top_value):
    longest = values.shape.index(max(values.shape))
    spots = []
    for shift in (0, 1):
        where = [jax.random.randint(jax.random.fold_in(key, axis), (), 0, length) for axis, length in enumerate(values.shape)]
        where[longest] = (where[longest] + shift) % values.shape[longest]
        spots.append(tuple(where))
    return values.at[spots[0]].set(least).at[spots[1]].set(top_value)


def block_levels(own_key, extent, split, least, high):
    def one(dim, shards_of):
        steps = jax.random.uniform(jax.random.fold_in(jax.random.fold_in(own_key, 6), dim), (shards_of,), jnp.float32, least / len(split), high / len(split))
        return jnp.repeat(jnp.exp(steps), extent[dim] // shards_of).reshape((-1,) + (1,) * (len(extent) - dim - 1))

    factor_of = one(*split[0])
    for cut in split[1:]:
        factor_of = factor_of * one(*cut)
    return factor_of


def bell_draw(own_key, shape, deviation, bound, split=(), held_as=jnp.bfloat16):
    values = jax.random.normal(own_key, shape, jnp.float32) * deviation
    if len(split) > 0:
        values = block_levels(own_key, shape, split, -0.22, 0.18) * values
    return jnp.clip(values, min=-bound, max=bound).astype(held_as)


def setup_inputs(seed: int = 0) -> dict:
    splits = jax.random.split(jax.random.key(seed), 8)
    populations = draw_populations(jax.random.fold_in(splits[7], 71), 0)
    thermal = draw_thermal(jax.random.fold_in(splits[7], 71), 0)
    velocity_prev = bell_draw(splits[2], (3, NX, NY, NZ), 0.1, 0.3, ((1, 16), (2, 4), (3, 4)), jnp.float32)
    solid = touch_ends((jax.random.randint(splits[3], (NX, NY, NZ), 0, 4) < 1).astype(jnp.int32), jax.random.fold_in(splits[3], 1), 0, 1)
    phase_ids = touch_ends(jax.random.randint(splits[4], (NX, NY, NZ), 0, PHASES), jax.random.fold_in(splits[4], 1), 0, PHASES - 1).astype(jnp.int32)
    conductivity = jnp.clip(jnp.exp(jax.random.uniform(splits[5], (PHASES,), jnp.float32, math.log(0.02), math.log(0.3))), 0.02, 0.3)
    rates = jnp.clip(jax.random.uniform(splits[6], (27,), jnp.float32, 0.7, 1.7), 0.7, 1.7)
    return dict(populations=populations, thermal=thermal, velocity_prev=velocity_prev, solid=solid, phase_ids=phase_ids, conductivity=conductivity, rates=rates)


HIGHEST = lax.Precision.HIGHEST
BUOYANCY = 0.03
REFERENCE_HEAT = 1.0
OFFSET_TABLE = [(number // 9 - 1, (number // 3) % 3 - 1, number % 3 - 1) for number in range(27)]
LATTICE_WEIGHTS = np.array([np.prod([2.0 / 3.0 if component == 0 else 1.0 / 6.0 for component in triple]) for triple in OFFSET_TABLE])
VANDERMONDE = np.array([[1.0, 1.0, 1.0], [-1.0, 0.0, 1.0], [1.0, 0.0, 1.0]])
VANDER_INVERSE = np.array([[0.0, -0.5, 0.5], [1.0, 0.0, -1.0], [0.0, 0.5, 0.5]])
MOMENT_MATRIX = np.kron(np.kron(VANDERMONDE, VANDERMONDE), VANDERMONDE)
MOMENT_INVERSE = np.kron(np.kron(VANDER_INVERSE, VANDER_INVERSE), VANDER_INVERSE)
RELAXED = np.array([0.0 if number in (0, 1, 3, 9) else 1.0 for number in range(27)])
SUMMING = np.concatenate([np.ones((1, 27)), 1.0 * np.array(OFFSET_TABLE).T], axis=0)
HEAT_WEIGHTS = np.array([0.25] + [0.125] * 6)
HEAT_TABLE = [(0, 0, 0), (1, 0, 0), (-1, 0, 0), (0, 1, 0), (0, -1, 0), (0, 0, 1), (0, 0, -1)]


def flow_state(flat, heat_flat):
    sums = jnp.dot(jnp.asarray(SUMMING, jnp.float32), flat, precision=HIGHEST)
    density = sums[0]
    force = BUOYANCY * (heat_flat - REFERENCE_HEAT)
    speed = jnp.stack([sums[1], sums[2], sums[3] + 0.5 * force]) / density
    return density, force, speed


def collide(popul, heat, rates):
    flat = popul.reshape(27, -1)
    density, force, speed = flow_state(flat, heat.reshape(-1))
    along = jnp.dot(jnp.asarray(SUMMING[1:].T, jnp.float32), speed, precision=HIGHEST)
    square = jnp.sum(speed * speed, axis=0)
    balance = density * jnp.asarray(LATTICE_WEIGHTS, jnp.float32)[:, None] * (1.0 + 3.0 * along + 4.5 * along * along - 1.5 * square)
    scaled = jnp.asarray(MOMENT_INVERSE, jnp.float32) * (rates * jnp.asarray(RELAXED, jnp.float32))[None, :]
    relax = jnp.dot(scaled, jnp.asarray(MOMENT_MATRIX, jnp.float32), precision=HIGHEST)
    post = flat - jnp.dot(relax, flat - balance, precision=HIGHEST) + jnp.asarray(MOMENT_INVERSE[:, 1], jnp.float32)[:, None] * force[None, :]
    return post.reshape(popul.shape)


def flow_speed(popul, heat, solid):
    density, force, speed = flow_state(popul.reshape(27, -1), heat.reshape(-1))
    return jnp.where(solid[None] == 0, speed.reshape((3,) + solid.shape), 0.0)


def heat_collide(heat_pops, speed, relax_time):
    total = jnp.sum(heat_pops, axis=0)
    still = jnp.zeros_like(speed[0])
    along = jnp.stack([still, speed[0], -speed[0], speed[1], -speed[1], speed[2], -speed[2]])
    balance = jnp.asarray(HEAT_WEIGHTS, jnp.float32)[:, None, None, None] * total[None] * (1.0 + 4.0 * along)
    return heat_pops - (heat_pops - balance) / relax_time[None]


def relaxation(phase_ids, conductivity):
    levels = jnp.arange(conductivity.shape[0], dtype=jnp.int32)
    chosen = jnp.sum(jnp.where(phase_ids[None] == levels[:, None, None, None], conductivity[:, None, None, None], 0.0), axis=0)
    return 0.5 + 4.0 * chosen


def stream_flow(post, popul, solid):
    fluid_cells = solid == 0
    layers = []
    for number in range(27):
        offset_triple = OFFSET_TABLE[number]
        arrived = jnp.roll(post[number], offset_triple, axis=(0, 1, 2))
        blocked = jnp.roll(solid, offset_triple, axis=(0, 1, 2)) != 0
        layers.append(jnp.where(fluid_cells, jnp.where(blocked, post[26 - number], arrived), popul[number]))
    return jnp.stack(layers)


def stream_heat(post):
    return jnp.stack([jnp.roll(post[number], HEAT_TABLE[number], axis=(0, 1, 2)) for number in range(7)])


def reference(populations, thermal, velocity_prev, solid, phase_ids, conductivity, rates):
    relax_time = relaxation(phase_ids, conductivity)
    speed = velocity_prev
    popul = populations
    heat_pops = thermal
    for window_number in range(WINDOWS):
        heat = jnp.sum(heat_pops, axis=0)
        for step_number in range(STEPS):
            popul = stream_flow(collide(popul, heat, rates), popul, solid)
        for step_number in range(STEPS):
            heat_pops = stream_heat(heat_collide(heat_pops, speed, relax_time))
        if window_number + 1 < WINDOWS:
            speed = flow_speed(popul, heat, solid)
    return popul, heat_pops
```

```python
import functools

import jax
import jax.numpy as jnp
import numpy as np
from jax import lax
from jax.experimental import pallas as pl
from jax.experimental.pallas import tpu as pltpu
from jax.sharding import PartitionSpec as P

STEPS = 4
WINDOWS = 2
BUOYANCY = 0.03
REFERENCE_HEAT = 1.0
MESH = pl.DeviceIdType.MESH
F32 = jnp.float32

RING = [(-1, -1), (-1, 0), "x-", (-1, 1), (0, 1), "y+", (1, 1), (1, 0), "x+", (1, -1), (0, -1), "y-", (0, 0), "0", "z+", "z-"]
THERMAL = {"0": (0, 0, 0), "x+": (1, 0, 0), "x-": (-1, 0, 0), "y+": (0, 1, 0), "y-": (0, -1, 0), "z+": (0, 0, 1), "z-": (0, 0, -1)}
HEAT_ORDER = ["0", "x+", "x-", "y+", "y-", "z+", "z-"]
VELOCITY = []
FLOW_AT = {}
HEAT_AT = {}
for entry in RING:
    if isinstance(entry, str):
        HEAT_AT[HEAT_ORDER.index(entry)] = len(VELOCITY)
        VELOCITY.append(THERMAL[entry])
    else:
        for c in (-1, 0, 1):
            FLOW_AT[entry + (c,)] = len(VELOCITY)
            VELOCITY.append(entry + (c,))
COUNT = len(VELOCITY)
FLOW = [(a, b, c) for a in (-1, 0, 1) for b in (-1, 0, 1) for c in (-1, 0, 1)]
X_GROUP = {1: (14, 24), -1: (0, 10)}
Y_GROUP = {1: [(7, 17)], -1: [(21, 28), (0, 3)]}
EDGE_GROUP = {(-1, -1): (0, 3), (-1, 1): (7, 10), (1, 1): (14, 17), (1, -1): (21, 24)}
X_SLOT, XH_SLOT, H_SLOT = 0, 1, 6
PLANES = 4
ROW = 8
SOURCE_ROW = {1: (15, 7), -1: (8, 16)}


def center(plane):
    return 32 * (plane + 1) % 128


def slot_of(a, plane):
    if plane < 0 or plane >= PLANES:
        return X_SLOT
    return 2 + (plane if a >= 0 else PLANES - 1 - plane)


def turn(value, amount):
    amount = amount % 128
    return pltpu.roll(value, amount, 1) if amount else value


MESSAGES = []
for (a, b), span in EDGE_GROUP.items():
    s, t = SOURCE_ROW[b]
    MESSAGES.append(((0, a, b), span, (5, 7), (0, 2), (s, s + 1), (t, t + 1)))
FIRST_X = len(MESSAGES)
for a in (1, -1):
    MESSAGES.append(((0, a, 0), X_GROUP[a], (5, 7), (0, 2), (ROW, ROW + 8), (ROW, ROW + 8)))
FIRST_Y = len(MESSAGES)
for b in (1, -1):
    s, t = SOURCE_ROW[b]
    for span in Y_GROUP[b]:
        MESSAGES.append(((0, 0, b), span, (2, 7), (2, 7), (s, s + 1), (t, t + 1)))

RELAXED = [m for m in [(p, q, r) for p in range(3) for q in range(3) for r in range(3)] if m not in ((0, 0, 0), (0, 0, 1), (0, 1, 0), (1, 0, 0))]
COEF = {}
for m in RELAXED:
    COEF[m, "keep"] = len(COEF)
    if m != (1, 1, 1):
        COEF[m, "gain"] = len(COEF)


def gain_scale(m):
    odd = sum(v == 1 for v in m)
    two = sum(v == 2 for v in m)
    return 3.0 ** (-(max(two - 1, 0) if odd == 0 else two))


def collide_flow(f, heat, coef):
    for axis in range(3):
        g = {}
        for one in (-1, 0, 1):
            for two in (-1, 0, 1):
                def at(v):
                    key = [one, two]
                    key.insert(axis, v)
                    return tuple(key)
                low, mid, high = f[at(-1)], f[at(0)], f[at(1)]
                both = high + low
                g[at(-1)] = both + mid
                g[at(0)] = high - low
                g[at(1)] = both
        f = g
    m = {(p, q, r): f[p - 1, q - 1, r - 1] for p in range(3) for q in range(3) for r in range(3)}
    rho, jx, jy, jz = m[0, 0, 0], m[1, 0, 0], m[0, 1, 0], m[0, 0, 1]
    force = BUOYANCY * (heat - REFERENCE_HEAT)
    flow_z = jz + 0.5 * force
    inverse = 1.0 / rho
    ux, uy, uz = jx * inverse, jy * inverse, flow_z * inverse
    third = rho * (1.0 / 3.0)
    xx, yy, zz = jx * ux, jy * uy, flow_z * uz
    square = {0: xx, 1: yy, 2: zz}
    flux = {0: jx, 1: jy, 2: flow_z}
    cross = {(0, 1): jx * uy, (0, 2): jx * uz, (1, 2): jy * uz}
    out = {}
    for k in RELAXED:
        odd = tuple(n for n in range(3) if k[n] == 1)
        if len(odd) == 3:
            out[k] = m[k] * coef(k, "keep")
            continue
        if len(odd) == 0:
            base = third
            for n in range(3):
                if k[n] == 2:
                    base = base + square[n]
        elif len(odd) == 1:
            base = flux[odd[0]]
        else:
            base = cross[odd]
        out[k] = m[k] * coef(k, "keep") + base * coef(k, "gain")
    out[0, 0, 0] = rho
    out[1, 0, 0] = 0.5 * jx
    out[0, 1, 0] = 0.5 * jy
    out[0, 0, 1] = 0.5 * (jz + force)
    f = {tuple(v - 1 for v in k): out[k] for k in out}
    for axis in range(3):
        g = {}
        for one in (-1, 0, 1):
            for two in (-1, 0, 1):
                def at(v):
                    key = [one, two]
                    key.insert(axis, v)
                    return tuple(key)
                zero, first, second = f[at(-1)], f[at(0)], f[at(1)]
                half = 0.5 * second
                g[at(-1)] = half - first
                g[at(0)] = zero - second
                g[at(1)] = half + first
        f = g
    return f, (inverse, jx, jy, jz)


def collide_heat(g, speed, omega):
    total = g[0]
    for k in range(1, 7):
        total = total + g[k]
    keep = 1.0 - omega
    part = omega * total * 0.125
    four = 4.0 * part
    out = [keep * g[0] + 2.0 * part]
    for d in range(3):
        push = four * speed[d]
        out.append(keep * g[1 + 2 * d] + (part + push))
        out.append(keep * g[2 + 2 * d] + (part - push))
    return out


def sum_heat(g):
    total = g[0]
    for k in range(1, 7):
        total = total + g[k]
    return total


def kernel(sizes, pop_ref, th_ref, vel_ref, solid_ref, ph_ref, cond_ref, rates_ref, fout, tout, post, stage, aux, coefs, hro, hrx, ar, ari, aps, apr, zs, zr, gs,
           send_sem, recv_sem, a_send, a_recv, z_send, z_recv, t_send, t_recv):
    me = {n: lax.axis_index(n) for n in sizes}
    names = list(sizes)

    def device(offset):
        return tuple(lax.rem(me[n] + (k + sizes[n]), sizes[n]) if k else me[n] for n, k in zip(names, offset))

    mine = me["grp"]
    barrier = pltpu.get_barrier_semaphore()
    others = [(0, a, b) for a in (-1, 0, 1) for b in (-1, 0, 1) if (a, b) != (0, 0)] + [(d, 0, 0) for d in (1, 2, 3)]
    for offset in others:
        pl.semaphore_signal(barrier, inc=1, device_id=device(offset), device_id_type=MESH)
    pl.semaphore_wait(barrier, len(others))

    lane = lax.broadcasted_iota(jnp.int32, (8, 128), 1)
    unit = (lane + 16) % 32

    def chunk(j):
        return pl.ds(pl.multiple_of(j * 128, 128), 128)

    a_copies = []
    for d in (2, 1, 3):
        target = lax.rem(mine + d, 4)
        to = device((d, 0, 0))
        for n, (src, dst) in enumerate(((th_ref.at[:, 0, :, chunk(target)], ar.at[mine]), (ph_ref.at[0, :, chunk(target)], ari.at[mine]))):
            a_copies.append(pltpu.make_async_remote_copy(src_ref=src, dst_ref=dst, send_sem=a_send.at[n, d - 1], recv_sem=a_recv.at[n, d - 1], device_id=to, device_id_type=MESH))
            a_copies[-1].start()
    for m in range(4):
        left, right = slice(128 * ((m + 3) % 4), 128 * ((m + 3) % 4) + 128), slice(128 * ((m + 1) % 4), 128 * ((m + 1) % 4) + 128)
        pack = None
        for k in range(8):
            if k < 7:
                both = jnp.where(lane < 64, th_ref[k, 0, :, right], th_ref[k, 0, :, left])
            else:
                both = jnp.where(lane < 64, ph_ref[0, :, right], ph_ref[0, :, left]).astype(F32)
            both = turn(both, 16 * k + 8)
            pack = both if pack is None else jnp.where(lane // 16 == k, both, pack)
        aps[m] = pack
    for d in (2, 1, 3):
        target = lax.rem(mine + d, 4)
        a_copies.append(pltpu.make_async_remote_copy(src_ref=aps.at[target], dst_ref=apr.at[mine], send_sem=a_send.at[2, d - 1], recv_sem=a_recv.at[2, d - 1], device_id=device((d, 0, 0)), device_id_type=MESH))
        a_copies[-1].start()
    apr[mine] = aps[mine]
    ar[mine] = th_ref[:, 0, :, chunk(mine)]
    ari[mine] = ph_ref[0, :, chunk(mine)]

    group = [(unit == unit) & (((lane - center(p) + 16) % 128) < 32) for p in range(4)]
    solid = [turn(solid_ref[p], center(p)) != 0 for p in range(4)]
    fields = [("f", key) for key in FLOW] + [("u", n) for n in range(3)]

    def merged(field):
        kind, key = field
        tile = None
        for p in range(4):
            if kind == "f":
                value = turn(pop_ref[FLOW.index(key), p], center(p))
                value = jnp.where(solid[p], jnp.nan, value)
                stage[FLOW_AT[key], p] = value
            else:
                value = turn(vel_ref[key, p], center(p))
                aux[1 + key, p] = value
            tile = value if tile is None else jnp.where(group[p], value, tile)
        return tile

    z_copies = []
    for n in range(15):
        one, two = merged(fields[2 * n]), merged(fields[2 * n + 1])
        zs[n] = jnp.where((unit >= 8) & (unit < 24), one, turn(two, 16))
        if n % 5 == 4:
            for side, d in ((0, 1), (1, -1)):
                z_copies.append(pltpu.make_async_remote_copy(src_ref=zs.at[n - 4 : n + 1], dst_ref=zr.at[side, n - 4 : n + 1], send_sem=z_send.at[side, n // 5], recv_sem=z_recv.at[side, n // 5], device_id=device((d, 0, 0)), device_id_type=MESH))
                z_copies[-1].start()

    for k in RELAXED:
        rate = rates_ref[9 * k[0] + 3 * k[1] + k[2]]
        half = 0.5 ** sum(v == 1 for v in k)
        coefs[COEF[k, "keep"]] = jnp.full((8, 128), (1.0 - rate) * half, F32)
        if (k, "gain") in COEF:
            coefs[COEF[k, "gain"]] = jnp.full((8, 128), rate * (half * gain_scale(k)), F32)

    def coef(k, kind):
        return coefs[COEF[k, kind]]

    for copy in a_copies:
        copy.wait()

    def omega_of(ids):
        level = jnp.full((8, 128), cond_ref[3], F32)
        for n in range(3):
            level = jnp.where(ids == n, cond_ref[n], level)
        return 1.0 / (0.5 + 4.0 * level)

    for p in range(4):
        g = [turn(ar[p, k], center(p)) for k in range(7)]
        for k in range(7):
            stage[HEAT_AT[k], p] = g[k]
        aux[0, p] = sum_heat(g)
        aux[4, p] = omega_of(turn(ari[p], center(p)))
    tiles = []
    for k in range(8):
        tile = None
        for p in range(4):
            value = turn(apr[p], center(p) - 16 * k - 8)
            tile = value if tile is None else jnp.where(group[p], value, tile)
        tiles.append(tile)
    for k in range(7):
        stage[HEAT_AT[k], 4] = tiles[k]
    aux[0, 4] = sum_heat(tiles[:7])
    aux[4, 4] = omega_of(tiles[7])

    for copy in z_copies:
        copy.wait()
    from_left = (unit // 8) % 2 == 1
    for n in range(15):
        both = jnp.where(from_left, zr[0, n], zr[1, n])
        for field, value in ((fields[2 * n], both), (fields[2 * n + 1], turn(both, -16))):
            kind, key = field
            if kind == "f":
                stage[FLOW_AT[key], 4] = value
            else:
                aux[1 + key, 4] = value

    def round_copies(parity):
        out = []
        for n, (offset, span, s_slots, t_slots, s_rows, t_rows) in enumerate(MESSAGES):
            out.append(pltpu.make_async_remote_copy(
                src_ref=post.at[parity, span[0] : span[1], s_slots[0] : s_slots[1], s_rows[0] : s_rows[1]],
                dst_ref=post.at[parity, span[0] : span[1], t_slots[0] : t_slots[1], t_rows[0] : t_rows[1]],
                send_sem=send_sem.at[parity, n], recv_sem=recv_sem.at[parity, n], device_id=device(offset), device_id_type=MESH))
        return out

    def own_slot(q, s):
        return H_SLOT if s == 4 else slot_of(VELOCITY[q][0], s)

    def put(parity, s, flow, heat):
        for key in FLOW:
            q = FLOW_AT[key]
            post[parity, q, own_slot(q, s), ROW : ROW + 8] = flow[key]
        for k in range(7):
            q = HEAT_AT[k]
            post[parity, q, own_slot(q, s), ROW : ROW + 8] = heat[k]

    def window(b):
        return slice(ROW - b, ROW - b + 8)

    def arrive(parity, q, s):
        a, b, c = VELOCITY[q]
        rows = window(b)
        amount = 32 * a + c
        if s < 4:
            base = turn(post[parity, q, slot_of(a, s - a), rows], amount)
            if c:
                halo = hro if 0 <= s - a < PLANES else hrx
                spot = center(s) if c == 1 else (center(s) - 1) % 128
                base = jnp.where(lane == spot, halo[q], base)
            return base
        base = post[parity, q, H_SLOT, rows]
        if a:
            outer = center(-1) if a == 1 else center(4)
            base = jnp.where((lane - outer + 16) % 128 < 32, post[parity, q, XH_SLOT, rows], base)
        if c:
            for p in range(4):
                spot = (center(p - a) - 1) % 128 if c == 1 else center(p - a)
                base = jnp.where(lane == spot, post[parity, q, slot_of(a, p - a), rows], base)
        return turn(base, amount)

    def flow_arrivals(parity, s):
        f = {}
        for key in FLOW:
            q = FLOW_AT[key]
            if key == (0, 0, 0):
                f[key] = post[parity, q, own_slot(q, s), ROW : ROW + 8]
                continue
            back = FLOW_AT[tuple(-v for v in key)]
            value = arrive(parity, q, s)
            f[key] = jnp.where(value != value, post[parity, back, own_slot(back, s), ROW : ROW + 8], value)
        return f

    def halo_rolls(parity, inner):
        for q in range(COUNT):
            a, b, c = VELOCITY[q]
            if c and inner:
                hro[q] = turn(post[parity, q, H_SLOT, window(b)], 32 * a + c)
            elif c and a:
                hrx[q] = turn(post[parity, q, XH_SLOT, window(b)], 32 * a + c)

    def start(parity, s, f, g, turned):
        heat_sum = sum_heat(g)
        old = aux[0, s]
        heat = old if turned is None else jnp.where(turned, heat_sum, old)
        flow, (inverse, jx, jy, jz) = collide_flow(f, heat, coef)
        speed = [aux[1 + n, s] for n in range(3)]
        if turned is not None:
            jz = jz + (0.5 * BUOYANCY) * (old - REFERENCE_HEAT)
            fresh = [j * inverse for j in (jx, jy, jz)]
            fresh = [jnp.where(v == v, v, 0.0) for v in fresh]
            speed = [jnp.where(turned, fresh[n], speed[n]) for n in range(3)]
            aux[0, s] = heat
            for n in range(3):
                aux[1 + n, s] = speed[n]
        put(parity, s, flow, collide_heat(g, speed, aux[4, s]))

    for s in (0, 3, 4, 1, 2):
        start(0, s, {key: stage[FLOW_AT[key], s] for key in FLOW}, [stage[HEAT_AT[k], s] for k in range(7)], None)
    for copy in round_copies(0):
        copy.start()

    def advance(step, carry):
        before = lax.rem(step + 1, 2)
        after = lax.rem(step, 2)
        turned = jnp.broadcast_to(step == STEPS, (8, 128))
        copies = round_copies(before)

        def pair(s):
            start(after, s, flow_arrivals(before, s), [arrive(before, HEAT_AT[k], s) for k in range(7)], turned)

        for copy in copies[FIRST_Y:]:
            copy.wait()
        halo_rolls(before, True)
        pair(1)
        pair(2)
        for copy in copies[:FIRST_Y]:
            copy.wait()
        halo_rolls(before, False)
        for s in (0, 3, 4):
            pair(s)
        for copy in round_copies(after):
            copy.start()
        return carry

    total = STEPS * WINDOWS
    lax.fori_loop(1, total, advance, 0)

    last = (total - 1) % 2
    copies = round_copies(last)
    for copy in copies:
        copy.wait()
    halo_rolls(last, True)
    halo_rolls(last, False)
    for p in range(4):
        for k in range(7):
            gs[p, k] = turn(arrive(last, HEAT_AT[k], p), -center(p))
    t_copies = []
    for d in (2, 1, 3):
        target = lax.rem(mine + d, 4)
        t_copies.append(pltpu.make_async_remote_copy(src_ref=gs.at[target], dst_ref=tout.at[:, 0, :, chunk(mine)], send_sem=t_send.at[d - 1], recv_sem=t_recv.at[d - 1], device_id=device((d, 0, 0)), device_id_type=MESH))
        t_copies[-1].start()
    tout[:, 0, :, chunk(mine)] = gs[mine]
    for p in range(4):
        f = flow_arrivals(last, p)
        for n, key in enumerate(FLOW):
            fout[n, p] = jnp.where(solid_ref[p] != 0, pop_ref[n, p], turn(f[key], -center(p)))
    for copy in t_copies:
        copy.wait()


def solution(mesh):
    sizes = dict(mesh.shape)

    def on_device(populations, thermal, velocity_prev, solid, phase_ids, conductivity, rates):
        vmem = pl.BlockSpec(memory_space=pltpu.VMEM)
        smem = pl.BlockSpec(memory_space=pltpu.SMEM)
        tile = (8, 128)
        return pl.pallas_call(
            functools.partial(kernel, sizes),
            out_shape=(jax.ShapeDtypeStruct(populations.shape, F32), jax.ShapeDtypeStruct(thermal.shape, F32)),
            in_specs=[vmem] * 5 + [smem] * 2,
            out_specs=(vmem, vmem),
            scratch_shapes=[
                pltpu.VMEM((2, COUNT, 7, 24, 128), F32),
                pltpu.VMEM((COUNT, 5) + tile, F32),
                pltpu.VMEM((5, 5) + tile, F32),
                pltpu.VMEM((len(COEF),) + tile, F32),
                pltpu.VMEM((COUNT,) + tile, F32),
                pltpu.VMEM((COUNT,) + tile, F32),
                pltpu.VMEM((4, 7) + tile, F32),
                pltpu.VMEM((4,) + tile, jnp.int32),
                pltpu.VMEM((4,) + tile, F32),
                pltpu.VMEM((4,) + tile, F32),
                pltpu.VMEM((15,) + tile, F32),
                pltpu.VMEM((2, 15) + tile, F32),
                pltpu.VMEM((4, 7) + tile, F32),
                pltpu.SemaphoreType.DMA((2, len(MESSAGES))),
                pltpu.SemaphoreType.DMA((2, len(MESSAGES))),
                pltpu.SemaphoreType.DMA((3, 3)),
                pltpu.SemaphoreType.DMA((3, 3)),
                pltpu.SemaphoreType.DMA((2, 3)),
                pltpu.SemaphoreType.DMA((2, 3)),
                pltpu.SemaphoreType.DMA((3,)),
                pltpu.SemaphoreType.DMA((3,)),
            ],
            compiler_params=pltpu.CompilerParams(collective_id=0, has_side_effects=True, vmem_limit_bytes=48 * 1024 * 1024),
        )(populations, thermal, velocity_prev, solid, phase_ids, conductivity, rates)

    in_specs = (
        P(None, "gx", "gy", "grp"),
        P(None, ("gx", "grp"), "gy", None),
        P(None, "gx", "gy", "grp"),
        P("gx", "gy", "grp"),
        P(("gx", "grp"), "gy", None),
        P(),
        P(),
    )
    out_specs = (P(None, "gx", "gy", "grp"), P(None, ("gx", "grp"), "gy", None))
    return jax.shard_map(on_device, mesh=mesh, in_specs=in_specs, out_specs=out_specs, check_vma=False)
```

```python
import functools

import jax
import jax.numpy as jnp
import numpy as np
from jax import lax
from jax.experimental import pallas as pl
from jax.experimental.pallas import tpu as pltpu
from jax.sharding import PartitionSpec as P

STEPS = 4
WINDOWS = 2
BUOYANCY = 0.03
REFERENCE_HEAT = 1.0
MESH = pl.DeviceIdType.MESH
F32 = jnp.float32

RING = [(-1, -1), (-1, 0), "x-", (-1, 1), (0, 1), "y+", (1, 1), (1, 0), "x+", (1, -1), (0, -1), "y-", (0, 0), "0", "z+", "z-"]
THERMAL = {"0": (0, 0, 0), "x+": (1, 0, 0), "x-": (-1, 0, 0), "y+": (0, 1, 0), "y-": (0, -1, 0), "z+": (0, 0, 1), "z-": (0, 0, -1)}
HOME_ORDER = [0, 5, 6, 3, 4, 1, 2]
HEAT_ORDER = ["0", "x+", "x-", "y+", "y-", "z+", "z-"]
VELOCITY = []
FLOW_AT = {}
HEAT_AT = {}
for entry in RING:
    if isinstance(entry, str):
        HEAT_AT[HEAT_ORDER.index(entry)] = len(VELOCITY)
        VELOCITY.append(THERMAL[entry])
    else:
        for c in (-1, 0, 1):
            FLOW_AT[entry + (c,)] = len(VELOCITY)
            VELOCITY.append(entry + (c,))
COUNT = len(VELOCITY)
FLOW = [(a, b, c) for a in (-1, 0, 1) for b in (-1, 0, 1) for c in (-1, 0, 1)]
X_GROUP = {1: (14, 24), -1: (0, 10)}
Y_GROUP = {1: [(7, 17)], -1: [(21, 28), (0, 3)]}
EDGE_GROUP = {(-1, -1): (0, 3), (-1, 1): (7, 10), (1, 1): (14, 17), (1, -1): (21, 24)}
X_SLOT, XH_SLOT, H_SLOT = 0, 1, 6
PLANES = 4
ROW = 8
SOURCE_ROW = {1: (15, 7), -1: (8, 16)}


def center(plane):
    return 32 * (plane + 1) % 128


def slot_of(a, plane):
    if plane < 0 or plane >= PLANES:
        return X_SLOT
    return 2 + (plane if a >= 0 else PLANES - 1 - plane)


def turn(value, amount):
    amount = amount % 128
    return pltpu.roll(value, amount, 1) if amount else value


MESSAGES = []
for (a, b), span in EDGE_GROUP.items():
    s, t = SOURCE_ROW[b]
    MESSAGES.append(((0, a, b), span, (5, 7), (0, 2), (s, s + 1), (t, t + 1)))
FIRST_X = len(MESSAGES)
for a in (1, -1):
    MESSAGES.append(((0, a, 0), X_GROUP[a], (5, 7), (0, 2), (ROW, ROW + 8), (ROW, ROW + 8)))
FIRST_Y = len(MESSAGES)
for b in (1, -1):
    s, t = SOURCE_ROW[b]
    for span in Y_GROUP[b]:
        MESSAGES.append(((0, 0, b), span, (2, 7), (2, 7), (s, s + 1), (t, t + 1)))

RELAXED = [m for m in [(p, q, r) for p in range(3) for q in range(3) for r in range(3)] if m not in ((0, 0, 0), (0, 0, 1), (0, 1, 0), (1, 0, 0))]
COEF = {}
for m in RELAXED:
    COEF[m, "keep"] = len(COEF)
    if m != (1, 1, 1):
        COEF[m, "gain"] = len(COEF)


def gain_scale(m):
    odd = sum(v == 1 for v in m)
    two = sum(v == 2 for v in m)
    return 3.0 ** (-(max(two - 1, 0) if odd == 0 else two))


def collide_flow(f, heat, coef):
    for axis in range(3):
        g = {}
        for one in (-1, 0, 1):
            for two in (-1, 0, 1):
                def at(v):
                    key = [one, two]
                    key.insert(axis, v)
                    return tuple(key)
                low, mid, high = f[at(-1)], f[at(0)], f[at(1)]
                both = high + low
                g[at(-1)] = both + mid
                g[at(0)] = high - low
                g[at(1)] = both
        f = g
    m = {(p, q, r): f[p - 1, q - 1, r - 1] for p in range(3) for q in range(3) for r in range(3)}
    rho, jx, jy, jz = m[0, 0, 0], m[1, 0, 0], m[0, 1, 0], m[0, 0, 1]
    force = BUOYANCY * (heat - REFERENCE_HEAT)
    flow_z = jz + 0.5 * force
    inverse = 1.0 / rho
    ux, uy, uz = jx * inverse, jy * inverse, flow_z * inverse
    third = rho * (1.0 / 3.0)
    xx, yy, zz = jx * ux, jy * uy, flow_z * uz
    square = {0: xx, 1: yy, 2: zz}
    flux = {0: jx, 1: jy, 2: flow_z}
    cross = {(0, 1): jx * uy, (0, 2): jx * uz, (1, 2): jy * uz}
    out = {}
    for k in RELAXED:
        odd = tuple(n for n in range(3) if k[n] == 1)
        if len(odd) == 3:
            out[k] = m[k] * coef(k, "keep")
            continue
        if len(odd) == 0:
            base = third
            for n in range(3):
                if k[n] == 2:
                    base = base + square[n]
        elif len(odd) == 1:
            base = flux[odd[0]]
        else:
            base = cross[odd]
        out[k] = m[k] * coef(k, "keep") + base * coef(k, "gain")
    out[0, 0, 0] = rho
    out[1, 0, 0] = 0.5 * jx
    out[0, 1, 0] = 0.5 * jy
    out[0, 0, 1] = 0.5 * (jz + force)
    f = {tuple(v - 1 for v in k): out[k] for k in out}
    for axis in range(3):
        g = {}
        for one in (-1, 0, 1):
            for two in (-1, 0, 1):
                def at(v):
                    key = [one, two]
                    key.insert(axis, v)
                    return tuple(key)
                zero, first, second = f[at(-1)], f[at(0)], f[at(1)]
                half = 0.5 * second
                g[at(-1)] = half - first
                g[at(0)] = zero - second
                g[at(1)] = half + first
        f = g
    return f, (inverse, jx, jy, jz)


def collide_heat(g, speed, omega):
    total = g[0]
    for k in range(1, 7):
        total = total + g[k]
    keep = 1.0 - omega
    part = omega * total * 0.125
    four = 4.0 * part
    out = [keep * g[0] + 2.0 * part]
    for d in range(3):
        push = four * speed[d]
        out.append(keep * g[1 + 2 * d] + (part + push))
        out.append(keep * g[2 + 2 * d] + (part - push))
    return out


def sum_heat(g):
    total = g[0]
    for k in range(1, 7):
        total = total + g[k]
    return total


def kernel(sizes, pop_in, th_in, vel_in, solid_in, ph_in, cond_in, rates_in, fout, tout, pop_ref, th_ref, vel_ref, solid_ref, ph_ref, cond_ref, rates_ref,
           post, stage, aux, coefs, hro, hrx, ar, ari, aps, apr, zs, zr, gs, own, own_row,
           in_sem, send_sem, recv_sem, a_send, a_recv, z_send, z_recv, t_send, t_recv):
    loads = [pltpu.make_async_copy(src, dst, in_sem.at[n]) for n, (src, dst) in enumerate((
        (th_in, th_ref), (ph_in, ph_ref), (pop_in, pop_ref), (solid_in, solid_ref), (vel_in, vel_ref), (rates_in, rates_ref), (cond_in, cond_ref)))]
    for copy in loads:
        copy.start()
    me = {n: lax.axis_index(n) for n in sizes}
    names = list(sizes)

    def device(offset):
        return tuple(lax.rem(me[n] + (k + sizes[n]), sizes[n]) if k else me[n] for n, k in zip(names, offset))

    mine = me["grp"]
    barrier = pltpu.get_barrier_semaphore()
    others = [(0, a, b) for a in (-1, 0, 1) for b in (-1, 0, 1) if (a, b) != (0, 0)] + [(d, 0, 0) for d in (1, 2, 3)]
    for offset in others:
        pl.semaphore_signal(barrier, inc=1, device_id=device(offset), device_id_type=MESH)

    lane = lax.broadcasted_iota(jnp.int32, (8, 128), 1)
    unit = (lane + 16) % 32

    def chunk(j):
        return pl.ds(pl.multiple_of(j * 128, 128), 128)

    loads[0].wait()
    loads[1].wait()
    for m in range(4):
        left, right = slice(128 * ((m + 3) % 4), 128 * ((m + 3) % 4) + 128), slice(128 * ((m + 1) % 4), 128 * ((m + 1) % 4) + 128)
        pack = None
        for k in range(8):
            if k < 7:
                both = jnp.where(lane < 64, th_ref[k, 0, :, right], th_ref[k, 0, :, left])
            else:
                both = jnp.where(lane < 64, ph_ref[0, :, right], ph_ref[0, :, left]).astype(F32)
            both = turn(both, 16 * k + 8)
            pack = both if pack is None else jnp.where(lane // 16 == k, both, pack)
        aps[m] = pack
    apr[mine] = aps[mine]
    ar[mine] = th_ref[:, 0, :, chunk(mine)]
    ari[mine] = ph_ref[0, :, chunk(mine)]
    pl.semaphore_wait(barrier, len(others))
    a_copies = []
    for d in (2, 1, 3):
        target = lax.rem(mine + d, 4)
        to = device((d, 0, 0))
        for n, (src, dst) in enumerate(((th_ref.at[:, 0, :, chunk(target)], ar.at[mine]), (ph_ref.at[0, :, chunk(target)], ari.at[mine]), (aps.at[target], apr.at[mine]))):
            a_copies.append(pltpu.make_async_remote_copy(src_ref=src, dst_ref=dst, send_sem=a_send.at[n, d - 1], recv_sem=a_recv.at[n, d - 1], device_id=to, device_id_type=MESH))
            a_copies[-1].start()

    group = [(unit == unit) & (((lane - center(p) + 16) % 128) < 32) for p in range(4)]
    for copy in loads[2:5]:
        copy.wait()
    solid = [turn(solid_ref[p], center(p)) != 0 for p in range(4)]
    fields = [("f", key) for key in FLOW] + [("u", n) for n in range(3)]

    def merged(field):
        kind, key = field
        tile = None
        for p in range(4):
            if kind == "f":
                value = turn(pop_ref[FLOW.index(key), p], center(p))
                value = jnp.where(solid[p], jnp.nan, value)
                stage[FLOW_AT[key], p] = value
            else:
                value = turn(vel_ref[key, p], center(p))
                aux[1 + key, p] = value
            tile = value if tile is None else jnp.where(group[p], value, tile)
        return tile

    z_copies = []
    for n in range(8):
        low, high = None, None
        for k, field in enumerate(fields[4 * n : 4 * n + 4]):
            value = turn(merged(field), 8 * k - 8)
            low = value if low is None else jnp.where(unit // 8 == k, value, low)
            high = value if high is None else jnp.where(unit // 8 == (k + 1) % 4, value, high)
        zs[0, n] = low
        zs[1, n] = high
        if n % 4 == 3:
            for side, d in ((0, 1), (1, -1)):
                z_copies.append(pltpu.make_async_remote_copy(src_ref=zs.at[side, n - 3 : n + 1], dst_ref=zr.at[side, n - 3 : n + 1], send_sem=z_send.at[side, n // 4], recv_sem=z_recv.at[side, n // 4], device_id=device((d, 0, 0)), device_id_type=MESH))
                z_copies[-1].start()

    loads[5].wait()
    loads[6].wait()
    for k in RELAXED:
        rate = rates_ref[9 * k[0] + 3 * k[1] + k[2]]
        half = 0.5 ** sum(v == 1 for v in k)
        coefs[COEF[k, "keep"]] = jnp.full((8, 128), (1.0 - rate) * half, F32)
        if (k, "gain") in COEF:
            coefs[COEF[k, "gain"]] = jnp.full((8, 128), rate * (half * gain_scale(k)), F32)

    def coef(k, kind):
        return coefs[COEF[k, kind]]

    for copy in a_copies:
        copy.wait()

    def omega_of(ids):
        level = jnp.full((8, 128), cond_ref[3], F32)
        for n in range(3):
            level = jnp.where(ids == n, cond_ref[n], level)
        return 1.0 / (0.5 + 4.0 * level)

    for p in range(4):
        g = [turn(ar[p, k], center(p)) for k in range(7)]
        for k in range(7):
            stage[HEAT_AT[k], p] = g[k]
        aux[0, p] = sum_heat(g)
        aux[4, p] = omega_of(turn(ari[p], center(p)))
    tiles = []
    for k in range(8):
        tile = None
        for p in range(4):
            value = turn(apr[p], center(p) - 16 * k - 8)
            tile = value if tile is None else jnp.where(group[p], value, tile)
        tiles.append(tile)
    for k in range(7):
        stage[HEAT_AT[k], 4] = tiles[k]
    aux[0, 4] = sum_heat(tiles[:7])
    aux[4, 4] = omega_of(tiles[7])

    for copy in z_copies:
        copy.wait()
    for n in range(8):
        low, high = zr[0, n], zr[1, n]
        for k, (kind, key) in enumerate(fields[4 * n : 4 * n + 4]):
            value = turn(jnp.where(unit // 8 == k, low, high), 8 - 8 * k)
            if kind == "f":
                stage[FLOW_AT[key], 4] = value
            else:
                aux[1 + key, 4] = value

    def round_copies(parity):
        out = []
        for n, (offset, span, s_slots, t_slots, s_rows, t_rows) in enumerate(MESSAGES):
            out.append(pltpu.make_async_remote_copy(
                src_ref=post.at[parity, span[0] : span[1], s_slots[0] : s_slots[1], s_rows[0] : s_rows[1]],
                dst_ref=post.at[parity, span[0] : span[1], t_slots[0] : t_slots[1], t_rows[0] : t_rows[1]],
                send_sem=send_sem.at[parity, n], recv_sem=recv_sem.at[parity, n], device_id=device(offset), device_id_type=MESH))
        return out

    def own_slot(q, s):
        return H_SLOT if s == 4 else slot_of(VELOCITY[q][0], s)

    def put(parity, s, flow, heat):
        for key in FLOW:
            q = FLOW_AT[key]
            post[parity, q, own_slot(q, s), ROW : ROW + 8] = flow[key]
        for k in range(7):
            q = HEAT_AT[k]
            post[parity, q, own_slot(q, s), ROW : ROW + 8] = heat[k]

    def window(b):
        return slice(ROW - b, ROW - b + 8)

    def arrive(parity, q, s):
        a, b, c = VELOCITY[q]
        rows = window(b)
        amount = 32 * a + c
        if s < 4:
            base = turn(post[parity, q, slot_of(a, s - a), rows], amount)
            if c:
                halo = hro if 0 <= s - a < PLANES else hrx
                spot = center(s) if c == 1 else (center(s) - 1) % 128
                base = jnp.where(lane == spot, halo[q], base)
            return base
        base = post[parity, q, H_SLOT, rows]
        if a:
            outer = center(-1) if a == 1 else center(4)
            base = jnp.where((lane - outer + 16) % 128 < 32, post[parity, q, XH_SLOT, rows], base)
        if c:
            for p in range(4):
                spot = (center(p - a) - 1) % 128 if c == 1 else center(p - a)
                base = jnp.where(lane == spot, post[parity, q, slot_of(a, p - a), rows], base)
        return turn(base, amount)

    def flow_arrivals(parity, s):
        f = {}
        for key in FLOW:
            q = FLOW_AT[key]
            if key == (0, 0, 0):
                f[key] = post[parity, q, own_slot(q, s), ROW : ROW + 8]
                continue
            back = FLOW_AT[tuple(-v for v in key)]
            value = arrive(parity, q, s)
            f[key] = jnp.where(value != value, post[parity, back, own_slot(back, s), ROW : ROW + 8], value)
        return f

    def halo_rolls(parity, inner):
        for q in range(COUNT):
            a, b, c = VELOCITY[q]
            if c and inner:
                hro[q] = turn(post[parity, q, H_SLOT, window(b)], 32 * a + c)
            elif c and a:
                hrx[q] = turn(post[parity, q, XH_SLOT, window(b)], 32 * a + c)

    def start(parity, s, f, g, turned):
        heat_sum = sum_heat(g)
        old = aux[0, s]
        heat = old if turned is None else jnp.where(turned, heat_sum, old)
        flow, (inverse, jx, jy, jz) = collide_flow(f, heat, coef)
        speed = [aux[1 + n, s] for n in range(3)]
        if turned is not None:
            jz = jz + (0.5 * BUOYANCY) * (old - REFERENCE_HEAT)
            fresh = [j * inverse for j in (jx, jy, jz)]
            fresh = [jnp.where(v == v, v, 0.0) for v in fresh]
            speed = [jnp.where(turned, fresh[n], speed[n]) for n in range(3)]
            aux[0, s] = heat
            for n in range(3):
                aux[1 + n, s] = speed[n]
        put(parity, s, flow, collide_heat(g, speed, aux[4, s]))

    for s in (0, 3, 4, 1, 2):
        start(0, s, {key: stage[FLOW_AT[key], s] for key in FLOW}, [stage[HEAT_AT[k], s] for k in range(7)], None)
    for copy in round_copies(0):
        copy.start()

    total = STEPS * WINDOWS

    def home_copy(src, dst, n, d, to):
        return pltpu.make_async_remote_copy(src_ref=src, dst_ref=dst, send_sem=t_send.at[n, d], recv_sem=t_recv.at[n, d], device_id=to, device_id_type=MESH)

    def moved(n, by):
        return lax.rem(me[n] + by, sizes[n])

    def home_copies():
        out = []
        for d in (2, 3, 1, 0):
            j = lax.rem(mine + d, 4)
            up = moved("gx", jnp.where(j == 0, 1, 0))
            down = moved("gx", jnp.where(j == 3, sizes["gx"] - 1, 0))
            out.append((home_copy(gs.at[lax.rem(j + 3, 4), 5], own.at[mine, 5], 1, d, (j, up, me["gy"])), mine == 0 if d == 0 else None))
            out.append((home_copy(gs.at[lax.rem(j + 1, 4), 6], own.at[mine, 6], 2, d, (j, down, me["gy"])), mine == 3 if d == 0 else None))
            if d:
                out.append((home_copy(gs.at[j, 0:5], own.at[mine, 0:5], 0, d, (j, me["gx"], me["gy"])), None))
            out.append((home_copy(gs.at[j, 3, 7:8], own_row.at[mine, 0, 7:8], 3, d, (j, me["gx"], moved("gy", 1))), None))
            out.append((home_copy(gs.at[j, 4, 0:1], own_row.at[mine, 1, 0:1], 4, d, (j, me["gx"], moved("gy", sizes["gy"] - 1))), None))
        return out

    def perform(copies, what):
        for copy, only in copies:
            if only is None:
                what(copy)
            else:
                pl.when(only)(functools.partial(what, copy))

    def home_start(parity):
        for p in range(4):
            for n, k in enumerate(HOME_ORDER):
                q = HEAT_AT[k]
                gs[p, n] = turn(post[parity, q, own_slot(q, p), ROW : ROW + 8], -center(p))
        perform(home_copies(), lambda copy: copy.start())
        own[mine, 0:5] = gs[mine, 0:5]

        @pl.when(mine != 0)
        def _():
            own[mine, 5] = gs[lax.rem(mine + 3, 4), 5]

        @pl.when(mine != 3)
        def _():
            own[mine, 6] = gs[lax.rem(mine + 1, 4), 6]

    def advance(step, carry):
        before = lax.rem(step + 1, 2)
        after = lax.rem(step, 2)
        turned = jnp.broadcast_to(step == STEPS, (8, 128))
        copies = round_copies(before)

        def pair(s):
            start(after, s, flow_arrivals(before, s), [arrive(before, HEAT_AT[k], s) for k in range(7)], turned)

        for copy in copies[FIRST_Y:]:
            copy.wait()
        halo_rolls(before, True)
        pair(1)
        pair(2)
        for copy in copies[:FIRST_Y]:
            copy.wait()
        halo_rolls(before, False)
        for s in (0, 3, 4):
            pair(s)

        @pl.when(step == total - 1)
        def _():
            home_start(after)

        for copy in round_copies(after):
            copy.start()
        return carry

    lax.fori_loop(1, total, advance, 0)

    last = (total - 1) % 2
    copies = round_copies(last)
    for copy in copies:
        copy.wait()
    halo_rolls(last, True)
    halo_rolls(last, False)
    for p in range(4):
        f = flow_arrivals(last, p)
        for n, key in enumerate(FLOW):
            fout[n, p] = jnp.where(solid_ref[p] != 0, pop_ref[n, p], turn(f[key], -center(p)))
    perform(home_copies(), lambda copy: copy.wait())
    row = lax.broadcasted_iota(jnp.int32, (8, 128), 0)
    for n in range(4):
        tiles = {k: own[n, place] for place, k in enumerate(HOME_ORDER)}
        tiles[3] = pltpu.roll(jnp.where(row == 7, own_row[n, 0], tiles[3]), 1, 0)
        tiles[4] = pltpu.roll(jnp.where(row == 0, own_row[n, 1], tiles[4]), 7, 0)
        tiles[5] = turn(jnp.where(lane == 127, own[(n + 3) % 4, HOME_ORDER.index(5)], tiles[5]), 1)
        tiles[6] = turn(jnp.where(lane == 0, own[(n + 1) % 4, HOME_ORDER.index(6)], tiles[6]), -1)
        for k in range(7):
            tout[k, 0, :, 128 * n : 128 * n + 128] = tiles[k]


def solution(mesh):
    sizes = dict(mesh.shape)

    def on_device(populations, thermal, velocity_prev, solid, phase_ids, conductivity, rates):
        vmem = pl.BlockSpec(memory_space=pltpu.VMEM)
        hbm = pl.BlockSpec(memory_space=pltpu.HBM)
        tile = (8, 128)
        return pl.pallas_call(
            functools.partial(kernel, sizes),
            out_shape=(jax.ShapeDtypeStruct(populations.shape, F32), jax.ShapeDtypeStruct(thermal.shape, F32)),
            in_specs=[hbm] * 7,
            out_specs=(vmem, vmem),
            scratch_shapes=[pltpu.VMEM(v.shape, v.dtype) for v in (populations, thermal, velocity_prev, solid, phase_ids)]
            + [pltpu.SMEM(v.shape, v.dtype) for v in (conductivity, rates)]
            + [
                pltpu.VMEM((2, COUNT, 7, 24, 128), F32),
                pltpu.VMEM((COUNT, 5) + tile, F32),
                pltpu.VMEM((5, 5) + tile, F32),
                pltpu.VMEM((len(COEF),) + tile, F32),
                pltpu.VMEM((COUNT,) + tile, F32),
                pltpu.VMEM((COUNT,) + tile, F32),
                pltpu.VMEM((4, 7) + tile, F32),
                pltpu.VMEM((4,) + tile, jnp.int32),
                pltpu.VMEM((4,) + tile, F32),
                pltpu.VMEM((4,) + tile, F32),
                pltpu.VMEM((2, 8) + tile, F32),
                pltpu.VMEM((2, 8) + tile, F32),
                pltpu.VMEM((4, 7) + tile, F32),
                pltpu.VMEM((4, 7) + tile, F32),
                pltpu.VMEM((4, 2) + tile, F32),
                pltpu.SemaphoreType.DMA((7,)),
                pltpu.SemaphoreType.DMA((2, len(MESSAGES))),
                pltpu.SemaphoreType.DMA((2, len(MESSAGES))),
                pltpu.SemaphoreType.DMA((3, 3)),
                pltpu.SemaphoreType.DMA((3, 3)),
                pltpu.SemaphoreType.DMA((2, 2)),
                pltpu.SemaphoreType.DMA((2, 2)),
                pltpu.SemaphoreType.DMA((5, 4)),
                pltpu.SemaphoreType.DMA((5, 4)),
            ],
            compiler_params=pltpu.CompilerParams(collective_id=0, has_side_effects=True, vmem_limit_bytes=48 * 1024 * 1024),
        )(*[pltpu.with_memory_space_constraint(v, pltpu.HBM) for v in (populations, thermal, velocity_prev, solid, phase_ids, conductivity, rates)])

    in_specs = (
        P(None, "gx", "gy", "grp"),
        P(None, ("gx", "grp"), "gy", None),
        P(None, "gx", "gy", "grp"),
        P("gx", "gy", "grp"),
        P(("gx", "grp"), "gy", None),
        P(),
        P(),
    )
    out_specs = (P(None, "gx", "gy", "grp"), P(None, ("gx", "grp"), "gy", None))
    return jax.shard_map(on_device, mesh=mesh, in_specs=in_specs, out_specs=out_specs, check_vma=False)
```

```python
import functools

import jax
import jax.numpy as jnp
import numpy as np
from jax import lax
from jax.experimental import pallas as pl
from jax.experimental.pallas import tpu as pltpu
from jax.sharding import PartitionSpec as P

STEPS = 4
WINDOWS = 2
BUOYANCY = 0.03
REFERENCE_HEAT = 1.0
MESH = pl.DeviceIdType.MESH
F32 = jnp.float32

RING = [(-1, -1), (-1, 0), (-1, 1), (0, 1), (1, 1), (1, 0), (1, -1), (0, -1), (0, 0), "0", "x+", "x-", "y+", "y-", "z+", "z-"]
THERMAL = {"0": (0, 0, 0), "x+": (1, 0, 0), "x-": (-1, 0, 0), "y+": (0, 1, 0), "y-": (0, -1, 0), "z+": (0, 0, 1), "z-": (0, 0, -1)}
HOME_ORDER = [0, 5, 6, 3, 4, 1, 2]
HEAT_ORDER = ["0", "x+", "x-", "y+", "y-", "z+", "z-"]
VELOCITY = []
FLOW_AT = {}
HEAT_AT = {}
for entry in RING:
    if isinstance(entry, str):
        HEAT_AT[HEAT_ORDER.index(entry)] = len(VELOCITY)
        VELOCITY.append(THERMAL[entry])
    else:
        for c in (-1, 0, 1):
            FLOW_AT[entry + (c,)] = len(VELOCITY)
            VELOCITY.append(entry + (c,))
COUNT = len(VELOCITY)
FLOW = [(a, b, c) for a in (-1, 0, 1) for b in (-1, 0, 1) for c in (-1, 0, 1)]
X_GROUP = {-1: (0, 9), 1: (12, 21)}
Y_GROUP = {1: [(6, 15)], -1: [(18, 24), (0, 3)]}
EDGE_GROUP = {(-1, -1): (0, 3), (-1, 1): (6, 9), (1, 1): (12, 15), (1, -1): (18, 21)}
X_SLOT, XH_SLOT, H_SLOT = 0, 1, 6
PLANES = 4
ROW = 8
SOURCE_ROW = {1: (15, 7), -1: (8, 16)}


def center(plane):
    return 32 * (plane + 1) % 128


def slot_of(a, plane):
    if plane < 0 or plane >= PLANES:
        return X_SLOT
    return 2 + (plane if a >= 0 else PLANES - 1 - plane)


def turn(value, amount):
    amount = amount % 128
    return pltpu.roll(value, amount, 1) if amount else value


MESSAGES = []
for (a, b), span in EDGE_GROUP.items():
    s, t = SOURCE_ROW[b]
    MESSAGES.append(((0, a, b), span, (5, 7), (0, 2), (s, s + 1), (t, t + 1)))
FIRST_X = len(MESSAGES)
for a in (1, -1):
    MESSAGES.append(((0, a, 0), X_GROUP[a], (5, 7), (0, 2), (ROW, ROW + 8), (ROW, ROW + 8)))
FIRST_Y = len(MESSAGES)
for b in (1, -1):
    s, t = SOURCE_ROW[b]
    for span in Y_GROUP[b]:
        MESSAGES.append(((0, 0, b), span, (2, 7), (2, 7), (s, s + 1), (t, t + 1)))

FIRST_HEAT = len(MESSAGES)
for a in (1, -1):
    q = HEAT_AT[HEAT_ORDER.index("x+" if a == 1 else "x-")]
    MESSAGES.append(((0, a, 0), (q, q + 1), (5, 7), (0, 2), (ROW, ROW + 8), (ROW, ROW + 8)))
for b in (1, -1):
    q = HEAT_AT[HEAT_ORDER.index("y+" if b == 1 else "y-")]
    s, t = SOURCE_ROW[b]
    MESSAGES.append(((0, 0, b), (q, q + 1), (2, 7), (2, 7), (s, s + 1), (t, t + 1)))

RELAXED = [m for m in [(p, q, r) for p in range(3) for q in range(3) for r in range(3)] if m not in ((0, 0, 0), (0, 0, 1), (0, 1, 0), (1, 0, 0))]
COEF = {}
for m in RELAXED:
    COEF[m, "keep"] = len(COEF)
    if m != (1, 1, 1):
        COEF[m, "gain"] = len(COEF)


def gain_scale(m):
    odd = sum(v == 1 for v in m)
    two = sum(v == 2 for v in m)
    return 3.0 ** (-(max(two - 1, 0) if odd == 0 else two))


def collide_flow(f, heat, coef):
    for axis in range(3):
        g = {}
        for one in (-1, 0, 1):
            for two in (-1, 0, 1):
                def at(v):
                    key = [one, two]
                    key.insert(axis, v)
                    return tuple(key)
                low, mid, high = f[at(-1)], f[at(0)], f[at(1)]
                both = high + low
                g[at(-1)] = both + mid
                g[at(0)] = high - low
                g[at(1)] = both
        f = g
    m = {(p, q, r): f[p - 1, q - 1, r - 1] for p in range(3) for q in range(3) for r in range(3)}
    rho, jx, jy, jz = m[0, 0, 0], m[1, 0, 0], m[0, 1, 0], m[0, 0, 1]
    force = BUOYANCY * (heat - REFERENCE_HEAT)
    flow_z = jz + 0.5 * force
    inverse = 1.0 / rho
    ux, uy, uz = jx * inverse, jy * inverse, flow_z * inverse
    third = rho * (1.0 / 3.0)
    xx, yy, zz = jx * ux, jy * uy, flow_z * uz
    square = {0: xx, 1: yy, 2: zz}
    flux = {0: jx, 1: jy, 2: flow_z}
    cross = {(0, 1): jx * uy, (0, 2): jx * uz, (1, 2): jy * uz}
    out = {}
    for k in RELAXED:
        odd = tuple(n for n in range(3) if k[n] == 1)
        if len(odd) == 3:
            out[k] = m[k] * coef(k, "keep")
            continue
        if len(odd) == 0:
            base = third
            for n in range(3):
                if k[n] == 2:
                    base = base + square[n]
        elif len(odd) == 1:
            base = flux[odd[0]]
        else:
            base = cross[odd]
        out[k] = m[k] * coef(k, "keep") + base * coef(k, "gain")
    out[0, 0, 0] = rho
    out[1, 0, 0] = 0.5 * jx
    out[0, 1, 0] = 0.5 * jy
    out[0, 0, 1] = 0.5 * (jz + force)
    f = {tuple(v - 1 for v in k): out[k] for k in out}
    for axis in range(3):
        g = {}
        for one in (-1, 0, 1):
            for two in (-1, 0, 1):
                def at(v):
                    key = [one, two]
                    key.insert(axis, v)
                    return tuple(key)
                zero, first, second = f[at(-1)], f[at(0)], f[at(1)]
                half = 0.5 * second
                g[at(-1)] = half - first
                g[at(0)] = zero - second
                g[at(1)] = half + first
        f = g
    return f, (inverse, jx, jy, jz)


def collide_heat(g, speed, omega):
    total = g[0]
    for k in range(1, 7):
        total = total + g[k]
    keep = 1.0 - omega
    part = omega * total * 0.125
    four = 4.0 * part
    out = [keep * g[0] + 2.0 * part]
    for d in range(3):
        push = four * speed[d]
        out.append(keep * g[1 + 2 * d] + (part + push))
        out.append(keep * g[2 + 2 * d] + (part - push))
    return out


def sum_heat(g):
    total = g[0]
    for k in range(1, 7):
        total = total + g[k]
    return total


def kernel(sizes, pop_in, th_in, vel_in, solid_in, ph_in, cond_in, rates_in, fout, tout, pop_ref, th_ref, vel_ref, solid_ref, ph_ref, cond_ref, rates_ref,
           post, stage, aux, coefs, hro, hrx, ar, ari, aps, apr, zs, zr, gs, own, own_row,
           in_sem, send_sem, recv_sem, a_send, a_recv, z_send, z_recv, t_send, t_recv):
    loads = [pltpu.make_async_copy(src, dst, in_sem.at[n]) for n, (src, dst) in enumerate((
        (th_in, th_ref), (ph_in, ph_ref), (pop_in, pop_ref), (solid_in, solid_ref), (vel_in, vel_ref), (rates_in, rates_ref), (cond_in, cond_ref)))]
    for copy in loads:
        copy.start()
    me = {n: lax.axis_index(n) for n in sizes}
    names = list(sizes)

    def device(offset):
        return tuple(lax.rem(me[n] + (k + sizes[n]), sizes[n]) if k else me[n] for n, k in zip(names, offset))

    mine = me["grp"]
    barrier = pltpu.get_barrier_semaphore()
    others = [(0, a, b) for a in (-1, 0, 1) for b in (-1, 0, 1) if (a, b) != (0, 0)] + [(d, 0, 0) for d in (1, 2, 3)]
    for offset in others:
        pl.semaphore_signal(barrier, inc=1, device_id=device(offset), device_id_type=MESH)

    lane = lax.broadcasted_iota(jnp.int32, (8, 128), 1)
    unit = (lane + 16) % 32

    def chunk(j):
        return pl.ds(pl.multiple_of(j * 128, 128), 128)

    loads[0].wait()
    loads[1].wait()
    for m in range(4):
        left, right = slice(128 * ((m + 3) % 4), 128 * ((m + 3) % 4) + 128), slice(128 * ((m + 1) % 4), 128 * ((m + 1) % 4) + 128)
        pack = None
        for k in range(8):
            if k < 7:
                both = jnp.where(lane < 64, th_ref[k, 0, :, right], th_ref[k, 0, :, left])
            else:
                both = jnp.where(lane < 64, ph_ref[0, :, right], ph_ref[0, :, left]).astype(F32)
            both = turn(both, 16 * k + 8)
            pack = both if pack is None else jnp.where(lane // 16 == k, both, pack)
        aps[m, 0] = pack
        aps[m, 1] = sum_heat([th_ref[k, 0, :, 128 * m : 128 * m + 128] for k in range(7)])
    apr[mine] = aps[mine]
    ar[mine] = th_ref[:, 0, :, chunk(mine)]
    ari[mine] = ph_ref[0, :, chunk(mine)]

    group = [(unit == unit) & (((lane - center(p) + 16) % 128) < 32) for p in range(4)]
    for copy in loads[2:5]:
        copy.wait()
    solid = [turn(solid_ref[p], center(p)) != 0 for p in range(4)]
    fields = [("f", key) for key in FLOW] + [("u", n) for n in range(3)]

    def merged(field):
        kind, key = field
        tile = None
        for p in range(4):
            if kind == "f":
                value = turn(pop_ref[FLOW.index(key), p], center(p))
                value = jnp.where(solid[p], jnp.nan, value)
                stage[FLOW_AT[key], p] = value
            else:
                value = turn(vel_ref[key, p], center(p))
                aux[1 + key, p] = value
            tile = value if tile is None else jnp.where(group[p], value, tile)
        return tile

    for n in range(8):
        low, high = None, None
        for k, field in enumerate(fields[4 * n : 4 * n + 4]):
            value = turn(merged(field), 8 * k - 8)
            low = value if low is None else jnp.where(unit // 8 == k, value, low)
            high = value if high is None else jnp.where(unit // 8 == (k + 1) % 4, value, high)
        zs[0, n] = low
        zs[1, n] = high

    loads[5].wait()
    loads[6].wait()
    for k in RELAXED:
        rate = rates_ref[9 * k[0] + 3 * k[1] + k[2]]
        half = 0.5 ** sum(v == 1 for v in k)
        coefs[COEF[k, "keep"]] = jnp.full((8, 128), (1.0 - rate) * half, F32)
        if (k, "gain") in COEF:
            coefs[COEF[k, "gain"]] = jnp.full((8, 128), rate * (half * gain_scale(k)), F32)

    def coef(k, kind):
        return coefs[COEF[k, kind]]

    pl.semaphore_wait(barrier, len(others))
    first_copies, late_copies = [], []
    for d in (2, 1, 3):
        target = lax.rem(mine + d, 4)
        for n, (src, dst) in enumerate(((aps.at[target], apr.at[mine]), (th_ref.at[:, 0, :, chunk(target)], ar.at[mine]), (ph_ref.at[0, :, chunk(target)], ari.at[mine]))):
            copy = pltpu.make_async_remote_copy(src_ref=src, dst_ref=dst, send_sem=a_send.at[n, d - 1], recv_sem=a_recv.at[n, d - 1], device_id=device((d, 0, 0)), device_id_type=MESH)
            (late_copies if n else first_copies).append(copy)
    z_copies = [pltpu.make_async_remote_copy(src_ref=zs.at[side], dst_ref=zr.at[side], send_sem=z_send.at[side], recv_sem=z_recv.at[side], device_id=device((d, 0, 0)), device_id_type=MESH) for side, d in ((0, 1), (1, -1))]
    for copy in first_copies + z_copies:
        copy.start()

    def omega_of(ids):
        level = jnp.full((8, 128), cond_ref[3], F32)
        for n in range(3):
            level = jnp.where(ids == n, cond_ref[n], level)
        return 1.0 / (0.5 + 4.0 * level)

    for copy in first_copies:
        copy.wait()
    for p in range(4):
        aux[0, p] = turn(apr[p, 1], center(p))
    tiles = []
    for k in range(8):
        tile = None
        for p in range(4):
            value = turn(apr[p, 0], center(p) - 16 * k - 8)
            tile = value if tile is None else jnp.where(group[p], value, tile)
        tiles.append(tile)
    for k in range(7):
        stage[HEAT_AT[k], 4] = tiles[k]
    aux[0, 4] = sum_heat(tiles[:7])
    aux[4, 4] = omega_of(tiles[7])

    for copy in z_copies:
        copy.wait()
    for n in range(8):
        low, high = zr[0, n], zr[1, n]
        for k, (kind, key) in enumerate(fields[4 * n : 4 * n + 4]):
            value = turn(jnp.where(unit // 8 == k, low, high), 8 - 8 * k)
            if kind == "f":
                stage[FLOW_AT[key], 4] = value
            else:
                aux[1 + key, 4] = value

    def round_copies(parity):
        out = []
        for n, (offset, span, s_slots, t_slots, s_rows, t_rows) in enumerate(MESSAGES):
            out.append(pltpu.make_async_remote_copy(
                src_ref=post.at[parity, span[0] : span[1], s_slots[0] : s_slots[1], s_rows[0] : s_rows[1]],
                dst_ref=post.at[parity, span[0] : span[1], t_slots[0] : t_slots[1], t_rows[0] : t_rows[1]],
                send_sem=send_sem.at[parity, n], recv_sem=recv_sem.at[parity, n], device_id=device(offset), device_id_type=MESH))
        return out

    def own_slot(q, s):
        return H_SLOT if s == 4 else slot_of(VELOCITY[q][0], s)

    def put(parity, s, tiles):
        for q, value in tiles.items():
            post[parity, q, own_slot(q, s), ROW : ROW + 8] = value

    def window(b):
        return slice(ROW - b, ROW - b + 8)

    def arrive(parity, q, s):
        a, b, c = VELOCITY[q]
        rows = window(b)
        amount = 32 * a + c
        if s < 4:
            base = turn(post[parity, q, slot_of(a, s - a), rows], amount)
            if c:
                halo = hro if 0 <= s - a < PLANES else hrx
                spot = center(s) if c == 1 else (center(s) - 1) % 128
                base = jnp.where(lane == spot, halo[q], base)
            return base
        base = post[parity, q, H_SLOT, rows]
        if a:
            outer = center(-1) if a == 1 else center(4)
            base = jnp.where((lane - outer + 16) % 128 < 32, post[parity, q, XH_SLOT, rows], base)
        if c:
            for p in range(4):
                spot = (center(p - a) - 1) % 128 if c == 1 else center(p - a)
                base = jnp.where(lane == spot, post[parity, q, slot_of(a, p - a), rows], base)
        return turn(base, amount)

    def flow_arrival(parity, s, key):
        q = FLOW_AT[key]
        if key == (0, 0, 0):
            return post[parity, q, own_slot(q, s), ROW : ROW + 8]
        back = FLOW_AT[tuple(-v for v in key)]
        value = arrive(parity, q, s)
        return jnp.where(value != value, post[parity, back, own_slot(back, s), ROW : ROW + 8], value)

    def needs_edge(s, key):
        a, b, c = key
        return a != 0 and b != 0 and (s == 4 or (s == 0 and a == 1) or (s == 3 and a == -1))

    def halo_rolls(parity, kind):
        for q in range(27):
            a, b, c = VELOCITY[q]
            if c and kind == "own":
                hro[q] = turn(post[parity, q, H_SLOT, window(b)], 32 * a + c)
            elif c and a and kind == ("edge" if b else "face"):
                hrx[q] = turn(post[parity, q, XH_SLOT, window(b)], 32 * a + c)

    def start_flow(parity, s, f, g, turned):
        old = aux[0, s]
        heat = old if turned is None else jnp.where(turned, sum_heat(g), old)
        flow, (inverse, jx, jy, jz) = collide_flow(f, heat, coef)
        if turned is not None:
            jz = jz + (0.5 * BUOYANCY) * (old - REFERENCE_HEAT)
            fresh = [j * inverse for j in (jx, jy, jz)]
            fresh = [jnp.where(v == v, v, 0.0) for v in fresh]
            aux[0, s] = heat
            for n in range(3):
                aux[1 + n, s] = jnp.where(turned, fresh[n], aux[1 + n, s])
        put(parity, s, {FLOW_AT[key]: flow[key] for key in FLOW})

    def start_heat(parity, s, g):
        out = collide_heat(g, [aux[1 + n, s] for n in range(3)], aux[4, s])
        put(parity, s, {HEAT_AT[k]: out[k] for k in range(7)})

    def staged(s, keys):
        return {key: stage[FLOW_AT[key], s] for key in keys}

    def staged_heat(s):
        return [stage[HEAT_AT[k], s] for k in range(7)]

    def heat_arrivals(parity):
        for k in (5, 6):
            q = HEAT_AT[k]
            hro[q] = turn(post[parity, q, H_SLOT, ROW : ROW + 8], VELOCITY[q][2])
        for s in range(5):
            for k in range(7):
                stage[HEAT_AT[k], s] = arrive(parity, HEAT_AT[k], s)

    def heat_collide(parity):
        for s in range(5):
            start_heat(parity, s, staged_heat(s))

    first = round_copies(0)
    for s in (4, 0, 3):
        start_flow(0, s, staged(s, FLOW), None, None)
    for copy in first[:FIRST_X]:
        copy.start()
    for copy in late_copies:
        copy.start()
    for s in (1, 2):
        start_flow(0, s, staged(s, FLOW), None, None)
    for copy in first[FIRST_X:FIRST_HEAT]:
        copy.start()
    for copy in late_copies:
        copy.wait()
    for p in range(4):
        for k in range(7):
            stage[HEAT_AT[k], p] = turn(ar[p, k], center(p))
        aux[4, p] = omega_of(turn(ari[p], center(p)))
    heat_collide(0)
    for copy in first[FIRST_HEAT:]:
        copy.start()

    total = STEPS * WINDOWS

    def home_copy(src, dst, n, d, to):
        return pltpu.make_async_remote_copy(src_ref=src, dst_ref=dst, send_sem=t_send.at[n, d], recv_sem=t_recv.at[n, d], device_id=to, device_id_type=MESH)

    def moved(n, by):
        return lax.rem(me[n] + by, sizes[n])

    def home_copies():
        out = []
        for d in (2, 3, 1, 0):
            j = lax.rem(mine + d, 4)
            up = moved("gx", jnp.where(j == 0, 1, 0))
            down = moved("gx", jnp.where(j == 3, sizes["gx"] - 1, 0))
            out.append((home_copy(gs.at[lax.rem(j + 3, 4), 5], own.at[mine, 5], 1, d, (j, up, me["gy"])), mine == 0 if d == 0 else None))
            out.append((home_copy(gs.at[lax.rem(j + 1, 4), 6], own.at[mine, 6], 2, d, (j, down, me["gy"])), mine == 3 if d == 0 else None))
            if d:
                out.append((home_copy(gs.at[j, 0:5], own.at[mine, 0:5], 0, d, (j, me["gx"], me["gy"])), None))
            out.append((home_copy(gs.at[j, 3, 7:8], own_row.at[mine, 0, 7:8], 3, d, (j, me["gx"], moved("gy", 1))), None))
            out.append((home_copy(gs.at[j, 4, 0:1], own_row.at[mine, 1, 0:1], 4, d, (j, me["gx"], moved("gy", sizes["gy"] - 1))), None))
        return out

    def perform(copies, what):
        for copy, only in copies:
            if only is None:
                what(copy)
            else:
                pl.when(only)(functools.partial(what, copy))

    def home_start(parity):
        for p in range(4):
            for n, k in enumerate(HOME_ORDER):
                q = HEAT_AT[k]
                gs[p, n] = turn(post[parity, q, own_slot(q, p), ROW : ROW + 8], -center(p))
        perform(home_copies(), lambda copy: copy.start())
        own[mine, 0:5] = gs[mine, 0:5]

        @pl.when(mine != 0)
        def _():
            own[mine, 5] = gs[lax.rem(mine + 3, 4), 5]

        @pl.when(mine != 3)
        def _():
            own[mine, 6] = gs[lax.rem(mine + 1, 4), 6]

    def advance(step, carry):
        before = lax.rem(step + 1, 2)
        after = lax.rem(step, 2)
        turned = jnp.broadcast_to(step == STEPS, (8, 128))
        copies = round_copies(before)
        later = round_copies(after)

        def receive_heat():
            for copy in copies[FIRST_HEAT:]:
                copy.wait()
            heat_arrivals(before)

        def send_heat():
            heat_collide(after)
            for copy in later[FIRST_HEAT:]:
                copy.start()

        @pl.when(step == STEPS)
        def _():
            receive_heat()

        @pl.when(step > STEPS)
        def _():
            receive_heat()

            @pl.when(step < total - 1)
            def _():
                send_heat()

            @pl.when(step == total - 1)
            def _():
                heat_collide(after)
                home_start(after)

        for copy in copies[FIRST_Y:FIRST_HEAT]:
            copy.wait()
        halo_rolls(before, "own")
        for s in (1, 2):
            start_flow(after, s, {key: flow_arrival(before, s, key) for key in FLOW}, staged_heat(s), turned)
        for copy in copies[FIRST_X:FIRST_Y]:
            copy.wait()
        halo_rolls(before, "face")
        for s in (4, 0, 3):
            for key in FLOW:
                if not needs_edge(s, key):
                    stage[FLOW_AT[key], s] = flow_arrival(before, s, key)
        for copy in copies[:FIRST_X]:
            copy.wait()
        halo_rolls(before, "edge")
        for s in (4, 0, 3):
            f = {key: flow_arrival(before, s, key) if needs_edge(s, key) else stage[FLOW_AT[key], s] for key in FLOW}
            start_flow(after, s, f, staged_heat(s), turned)
            if s == 0:
                for copy in later[:2]:
                    copy.start()
            if s == 3:
                for copy in later[2:FIRST_X]:
                    copy.start()
        for copy in later[FIRST_X:FIRST_HEAT]:
            copy.start()

        @pl.when(step < STEPS)
        def _():
            receive_heat()
            send_heat()

        @pl.when(step == STEPS)
        def _():
            send_heat()

        return carry

    lax.fori_loop(1, total, advance, 0)

    last = (total - 1) % 2
    copies = round_copies(last)[:FIRST_HEAT]
    for copy in copies:
        copy.wait()
    for kind in ("own", "face", "edge"):
        halo_rolls(last, kind)
    for p in range(4):
        for n, key in enumerate(FLOW):
            fout[n, p] = jnp.where(solid_ref[p] != 0, pop_ref[n, p], turn(flow_arrival(last, p, key), -center(p)))
    perform(home_copies(), lambda copy: copy.wait())
    row = lax.broadcasted_iota(jnp.int32, (8, 128), 0)
    for n in range(4):
        tiles = {k: own[n, place] for place, k in enumerate(HOME_ORDER)}
        tiles[3] = pltpu.roll(jnp.where(row == 7, own_row[n, 0], tiles[3]), 1, 0)
        tiles[4] = pltpu.roll(jnp.where(row == 0, own_row[n, 1], tiles[4]), 7, 0)
        tiles[5] = turn(jnp.where(lane == 127, own[(n + 3) % 4, HOME_ORDER.index(5)], tiles[5]), 1)
        tiles[6] = turn(jnp.where(lane == 0, own[(n + 1) % 4, HOME_ORDER.index(6)], tiles[6]), -1)
        for k in range(7):
            tout[k, 0, :, 128 * n : 128 * n + 128] = tiles[k]


def write_out(flow, heat, fout, tout, sem):
    copies = [pltpu.make_async_copy(src, dst, sem.at[n]) for n, (src, dst) in enumerate(((flow, fout), (heat, tout)))]
    for copy in copies:
        copy.start()
    for copy in copies:
        copy.wait()


def solution(mesh):
    sizes = dict(mesh.shape)

    def on_device(populations, thermal, velocity_prev, solid, phase_ids, conductivity, rates):
        vmem = pl.BlockSpec(memory_space=pltpu.VMEM)
        hbm = pl.BlockSpec(memory_space=pltpu.HBM)
        tile = (8, 128)
        flow, heat = pl.pallas_call(
            functools.partial(kernel, sizes),
            out_shape=(jax.ShapeDtypeStruct(populations.shape, F32), jax.ShapeDtypeStruct(thermal.shape, F32)),
            in_specs=[hbm] * 7,
            out_specs=(vmem, vmem),
            scratch_shapes=[pltpu.VMEM(v.shape, v.dtype) for v in (populations, thermal, velocity_prev, solid, phase_ids)]
            + [pltpu.SMEM(v.shape, v.dtype) for v in (conductivity, rates)]
            + [
                pltpu.VMEM((2, COUNT, 7, 24, 128), F32),
                pltpu.VMEM((COUNT, 5) + tile, F32),
                pltpu.VMEM((5, 5) + tile, F32),
                pltpu.VMEM((len(COEF),) + tile, F32),
                pltpu.VMEM((COUNT,) + tile, F32),
                pltpu.VMEM((COUNT,) + tile, F32),
                pltpu.VMEM((4, 7) + tile, F32),
                pltpu.VMEM((4,) + tile, jnp.int32),
                pltpu.VMEM((4, 2) + tile, F32),
                pltpu.VMEM((4, 2) + tile, F32),
                pltpu.VMEM((2, 8) + tile, F32),
                pltpu.VMEM((2, 8) + tile, F32),
                pltpu.VMEM((4, 7) + tile, F32),
                pltpu.VMEM((4, 7) + tile, F32),
                pltpu.VMEM((4, 2) + tile, F32),
                pltpu.SemaphoreType.DMA((7,)),
                pltpu.SemaphoreType.DMA((2, len(MESSAGES))),
                pltpu.SemaphoreType.DMA((2, len(MESSAGES))),
                pltpu.SemaphoreType.DMA((3, 3)),
                pltpu.SemaphoreType.DMA((3, 3)),
                pltpu.SemaphoreType.DMA((2,)),
                pltpu.SemaphoreType.DMA((2,)),
                pltpu.SemaphoreType.DMA((5, 4)),
                pltpu.SemaphoreType.DMA((5, 4)),
            ],
            compiler_params=pltpu.CompilerParams(collective_id=0, has_side_effects=True, vmem_limit_bytes=48 * 1024 * 1024),
        )(*[pltpu.with_memory_space_constraint(v, pltpu.HBM) for v in (populations, thermal, velocity_prev, solid, phase_ids, conductivity, rates)])
        anywhere = pl.BlockSpec(memory_space=pl.ANY)
        return pl.pallas_call(
            write_out,
            out_shape=(jax.ShapeDtypeStruct(flow.shape, F32), jax.ShapeDtypeStruct(heat.shape, F32)),
            in_specs=[anywhere] * 2,
            out_specs=(anywhere, anywhere),
            scratch_shapes=[pltpu.SemaphoreType.DMA((2,))],
            compiler_params=pltpu.CompilerParams(vmem_limit_bytes=4 * 1024 * 1024),
        )(flow, heat)

    in_specs = (
        P(None, "gx", "gy", "grp"),
        P(None, ("gx", "grp"), "gy", None),
        P(None, "gx", "gy", "grp"),
        P("gx", "gy", "grp"),
        P(("gx", "grp"), "gy", None),
        P(),
        P(),
    )
    out_specs = (P(None, "gx", "gy", "grp"), P(None, ("gx", "grp"), "gy", None))
    return jax.shard_map(on_device, mesh=mesh, in_specs=in_specs, out_specs=out_specs, check_vma=False)
```

```python
import functools

import jax
import jax.numpy as jnp
import numpy as np
from jax import lax
from jax.experimental import pallas as pl
from jax.experimental.pallas import tpu as pltpu
from jax.sharding import PartitionSpec as P

STEPS = 4
WINDOWS = 2
BUOYANCY = 0.03
REFERENCE_HEAT = 1.0
MESH = pl.DeviceIdType.MESH
F32 = jnp.float32

RING = [(-1, -1), (-1, 0), (-1, 1), (0, 1), (1, 1), (1, 0), (1, -1), (0, -1), (0, 0), "0", "x+", "x-", "y+", "y-", "z+", "z-"]
THERMAL = {"0": (0, 0, 0), "x+": (1, 0, 0), "x-": (-1, 0, 0), "y+": (0, 1, 0), "y-": (0, -1, 0), "z+": (0, 0, 1), "z-": (0, 0, -1)}
HOME_ORDER = [0, 5, 6, 3, 4, 1, 2]
HEAT_ORDER = ["0", "x+", "x-", "y+", "y-", "z+", "z-"]
VELOCITY = []
FLOW_AT = {}
HEAT_AT = {}
for entry in RING:
    if isinstance(entry, str):
        HEAT_AT[HEAT_ORDER.index(entry)] = len(VELOCITY)
        VELOCITY.append(THERMAL[entry])
    else:
        for c in (-1, 0, 1):
            FLOW_AT[entry + (c,)] = len(VELOCITY)
            VELOCITY.append(entry + (c,))
COUNT = len(VELOCITY)
FLOW = [(a, b, c) for a in (-1, 0, 1) for b in (-1, 0, 1) for c in (-1, 0, 1)]
X_GROUP = {-1: (0, 9), 1: (12, 21)}
Y_GROUP = {1: [(6, 15)], -1: [(18, 24), (0, 3)]}
EDGE_GROUP = {(-1, -1): (0, 3), (-1, 1): (6, 9), (1, 1): (12, 15), (1, -1): (18, 21)}
X_SLOT, XH_SLOT, H_SLOT = 0, 1, 6
PLANES = 4
ROW = 8
SOURCE_ROW = {1: (15, 7), -1: (8, 16)}


def center(plane):
    return 32 * (plane + 1) % 128


def slot_of(a, plane):
    if plane < 0 or plane >= PLANES:
        return X_SLOT
    return 2 + (plane if a >= 0 else PLANES - 1 - plane)


def turn(value, amount):
    amount = amount % 128
    return pltpu.roll(value, amount, 1) if amount else value


MESSAGES = []
for (a, b), span in EDGE_GROUP.items():
    s, t = SOURCE_ROW[b]
    MESSAGES.append(((0, a, b), span, (5, 7), (0, 2), (s, s + 1), (t, t + 1)))
FIRST_X = len(MESSAGES)
for a in (1, -1):
    MESSAGES.append(((0, a, 0), X_GROUP[a], (5, 7), (0, 2), (ROW, ROW + 8), (ROW, ROW + 8)))
FIRST_Y = len(MESSAGES)
for b in (1, -1):
    s, t = SOURCE_ROW[b]
    for span in Y_GROUP[b]:
        MESSAGES.append(((0, 0, b), span, (2, 7), (2, 7), (s, s + 1), (t, t + 1)))

FIRST_HEAT = len(MESSAGES)
for a in (1, -1):
    q = HEAT_AT[HEAT_ORDER.index("x+" if a == 1 else "x-")]
    MESSAGES.append(((0, a, 0), (q, q + 1), (5, 7), (0, 2), (ROW, ROW + 8), (ROW, ROW + 8)))
for b in (1, -1):
    q = HEAT_AT[HEAT_ORDER.index("y+" if b == 1 else "y-")]
    s, t = SOURCE_ROW[b]
    MESSAGES.append(((0, 0, b), (q, q + 1), (2, 7), (2, 7), (s, s + 1), (t, t + 1)))

RELAXED = [m for m in [(p, q, r) for p in range(3) for q in range(3) for r in range(3)] if m not in ((0, 0, 0), (0, 0, 1), (0, 1, 0), (1, 0, 0))]
COEF = {}
for m in RELAXED:
    COEF[m, "keep"] = len(COEF)
    if m != (1, 1, 1):
        COEF[m, "gain"] = len(COEF)


def gain_scale(m):
    odd = sum(v == 1 for v in m)
    two = sum(v == 2 for v in m)
    return 3.0 ** (-(max(two - 1, 0) if odd == 0 else two))


def collide_flow(f, heat, coef):
    for axis in range(3):
        g = {}
        for one in (-1, 0, 1):
            for two in (-1, 0, 1):
                def at(v):
                    key = [one, two]
                    key.insert(axis, v)
                    return tuple(key)
                low, mid, high = f[at(-1)], f[at(0)], f[at(1)]
                both = high + low
                g[at(-1)] = both + mid
                g[at(0)] = high - low
                g[at(1)] = both
        f = g
    m = {(p, q, r): f[p - 1, q - 1, r - 1] for p in range(3) for q in range(3) for r in range(3)}
    rho, jx, jy, jz = m[0, 0, 0], m[1, 0, 0], m[0, 1, 0], m[0, 0, 1]
    force = BUOYANCY * (heat - REFERENCE_HEAT)
    flow_z = jz + 0.5 * force
    inverse = 1.0 / rho
    ux, uy, uz = jx * inverse, jy * inverse, flow_z * inverse
    third = rho * (1.0 / 3.0)
    xx, yy, zz = jx * ux, jy * uy, flow_z * uz
    square = {0: xx, 1: yy, 2: zz}
    flux = {0: jx, 1: jy, 2: flow_z}
    cross = {(0, 1): jx * uy, (0, 2): jx * uz, (1, 2): jy * uz}
    out = {}
    for k in RELAXED:
        odd = tuple(n for n in range(3) if k[n] == 1)
        if len(odd) == 3:
            out[k] = m[k] * coef(k, "keep")
            continue
        if len(odd) == 0:
            base = third
            for n in range(3):
                if k[n] == 2:
                    base = base + square[n]
        elif len(odd) == 1:
            base = flux[odd[0]]
        else:
            base = cross[odd]
        out[k] = m[k] * coef(k, "keep") + base * coef(k, "gain")
    out[0, 0, 0] = rho
    out[1, 0, 0] = 0.5 * jx
    out[0, 1, 0] = 0.5 * jy
    out[0, 0, 1] = 0.5 * (jz + force)
    f = {tuple(v - 1 for v in k): out[k] for k in out}
    for axis in range(3):
        g = {}
        for one in (-1, 0, 1):
            for two in (-1, 0, 1):
                def at(v):
                    key = [one, two]
                    key.insert(axis, v)
                    return tuple(key)
                zero, first, second = f[at(-1)], f[at(0)], f[at(1)]
                half = 0.5 * second
                g[at(-1)] = half - first
                g[at(0)] = zero - second
                g[at(1)] = half + first
        f = g
    return f, (inverse, jx, jy, jz)


def collide_heat(g, speed, omega):
    total = g[0]
    for k in range(1, 7):
        total = total + g[k]
    keep = 1.0 - omega
    part = omega * total * 0.125
    four = 4.0 * part
    out = [keep * g[0] + 2.0 * part]
    for d in range(3):
        push = four * speed[d]
        out.append(keep * g[1 + 2 * d] + (part + push))
        out.append(keep * g[2 + 2 * d] + (part - push))
    return out


def sum_heat(g):
    total = g[0]
    for k in range(1, 7):
        total = total + g[k]
    return total


def kernel(sizes, pop_in, th_in, vel_in, solid_in, ph_in, cond_in, rates_in, fout, tout, pop_ref, th_ref, vel_ref, solid_ref, ph_ref, cond_ref, rates_ref,
           post, stage, aux, coefs, hro, hrx, ar, ari, aps, apr, zs, zr, gs, own, own_row,
           in_sem, send_sem, recv_sem, a_send, a_recv, z_send, z_recv, t_send, t_recv):
    loads = [pltpu.make_async_copy(src, dst, in_sem.at[n]) for n, (src, dst) in enumerate((
        (th_in, th_ref), (ph_in, ph_ref), (pop_in, pop_ref), (solid_in, solid_ref), (vel_in, vel_ref), (rates_in, rates_ref), (cond_in, cond_ref)))]
    for copy in loads:
        copy.start()
    me = {n: lax.axis_index(n) for n in sizes}
    names = list(sizes)

    def device(offset):
        return tuple(lax.rem(me[n] + (k + sizes[n]), sizes[n]) if k else me[n] for n, k in zip(names, offset))

    mine = me["grp"]
    barrier = pltpu.get_barrier_semaphore()
    others = [(0, a, b) for a in (-1, 0, 1) for b in (-1, 0, 1) if (a, b) != (0, 0)] + [(d, 0, 0) for d in (1, 2, 3)]
    for offset in others:
        pl.semaphore_signal(barrier, inc=1, device_id=device(offset), device_id_type=MESH)

    lane = lax.broadcasted_iota(jnp.int32, (8, 128), 1)
    unit = (lane + 16) % 32

    def chunk(j):
        return pl.ds(pl.multiple_of(j * 128, 128), 128)

    loads[0].wait()
    loads[1].wait()
    for m in range(4):
        left, right = slice(128 * ((m + 3) % 4), 128 * ((m + 3) % 4) + 128), slice(128 * ((m + 1) % 4), 128 * ((m + 1) % 4) + 128)
        pack = None
        for k in range(8):
            if k < 7:
                both = jnp.where(lane < 64, th_ref[k, 0, :, right], th_ref[k, 0, :, left])
            else:
                both = jnp.where(lane < 64, ph_ref[0, :, right], ph_ref[0, :, left]).astype(F32)
            both = turn(both, 16 * k + 8)
            pack = both if pack is None else jnp.where(lane // 16 == k, both, pack)
        aps[m, 0] = pack
        aps[m, 1] = sum_heat([th_ref[k, 0, :, 128 * m : 128 * m + 128] for k in range(7)])
    apr[mine] = aps[mine]
    ar[mine] = th_ref[:, 0, :, chunk(mine)]
    ari[mine] = ph_ref[0, :, chunk(mine)]

    group = [(unit == unit) & (((lane - center(p) + 16) % 128) < 32) for p in range(4)]
    for copy in loads[2:5]:
        copy.wait()
    solid = [turn(solid_ref[p], center(p)) != 0 for p in range(4)]
    fields = [("f", key) for key in FLOW] + [("u", n) for n in range(3)]

    def merged(field):
        kind, key = field
        tile = None
        for p in range(4):
            if kind == "f":
                value = turn(pop_ref[FLOW.index(key), p], center(p))
                value = jnp.where(solid[p], jnp.nan, value)
                stage[FLOW_AT[key], p] = value
            else:
                value = turn(vel_ref[key, p], center(p))
                aux[1 + key, p] = value
            tile = value if tile is None else jnp.where(group[p], value, tile)
        return tile

    for n in range(8):
        low, high = None, None
        for k, field in enumerate(fields[4 * n : 4 * n + 4]):
            value = turn(merged(field), 8 * k - 8)
            low = value if low is None else jnp.where(unit // 8 == k, value, low)
            high = value if high is None else jnp.where(unit // 8 == (k + 1) % 4, value, high)
        zs[0, n] = low
        zs[1, n] = high

    loads[5].wait()
    loads[6].wait()
    for k in RELAXED:
        rate = rates_ref[9 * k[0] + 3 * k[1] + k[2]]
        half = 0.5 ** sum(v == 1 for v in k)
        coefs[COEF[k, "keep"]] = jnp.full((8, 128), (1.0 - rate) * half, F32)
        if (k, "gain") in COEF:
            coefs[COEF[k, "gain"]] = jnp.full((8, 128), rate * (half * gain_scale(k)), F32)

    def coef(k, kind):
        return coefs[COEF[k, kind]]

    pl.semaphore_wait(barrier, len(others))
    first_copies, late_copies = [], []
    for d in (2, 1, 3):
        target = lax.rem(mine + d, 4)
        for n, (src, dst) in enumerate(((aps.at[target], apr.at[mine]), (th_ref.at[:, 0, :, chunk(target)], ar.at[mine]), (ph_ref.at[0, :, chunk(target)], ari.at[mine]))):
            copy = pltpu.make_async_remote_copy(src_ref=src, dst_ref=dst, send_sem=a_send.at[n, d - 1], recv_sem=a_recv.at[n, d - 1], device_id=device((d, 0, 0)), device_id_type=MESH)
            (late_copies if n else first_copies).append(copy)
    z_copies = [pltpu.make_async_remote_copy(src_ref=zs.at[side], dst_ref=zr.at[side], send_sem=z_send.at[side], recv_sem=z_recv.at[side], device_id=device((d, 0, 0)), device_id_type=MESH) for side, d in ((0, 1), (1, -1))]
    for copy in first_copies + z_copies:
        copy.start()

    def omega_of(ids):
        level = jnp.full((8, 128), cond_ref[3], F32)
        for n in range(3):
            level = jnp.where(ids == n, cond_ref[n], level)
        return 1.0 / (0.5 + 4.0 * level)

    for copy in first_copies:
        copy.wait()
    for p in range(4):
        aux[0, p] = turn(apr[p, 1], center(p))
    tiles = []
    for k in range(8):
        tile = None
        for p in range(4):
            value = turn(apr[p, 0], center(p) - 16 * k - 8)
            tile = value if tile is None else jnp.where(group[p], value, tile)
        tiles.append(tile)
    for k in range(7):
        stage[HEAT_AT[k], 4] = tiles[k]
    aux[0, 4] = sum_heat(tiles[:7])
    aux[4, 4] = omega_of(tiles[7])

    for copy in z_copies:
        copy.wait()
    for n in range(8):
        low, high = zr[0, n], zr[1, n]
        for k, (kind, key) in enumerate(fields[4 * n : 4 * n + 4]):
            value = turn(jnp.where(unit // 8 == k, low, high), 8 - 8 * k)
            if kind == "f":
                stage[FLOW_AT[key], 4] = value
            else:
                aux[1 + key, 4] = value

    def round_copies(parity):
        out = []
        for n, (offset, span, s_slots, t_slots, s_rows, t_rows) in enumerate(MESSAGES):
            out.append(pltpu.make_async_remote_copy(
                src_ref=post.at[parity, span[0] : span[1], s_slots[0] : s_slots[1], s_rows[0] : s_rows[1]],
                dst_ref=post.at[parity, span[0] : span[1], t_slots[0] : t_slots[1], t_rows[0] : t_rows[1]],
                send_sem=send_sem.at[parity, n], recv_sem=recv_sem.at[parity, n], device_id=device(offset), device_id_type=MESH))
        return out

    def own_slot(q, s):
        return H_SLOT if s == 4 else slot_of(VELOCITY[q][0], s)

    def put(parity, s, tiles):
        for q, value in tiles.items():
            post[parity, q, own_slot(q, s), ROW : ROW + 8] = value

    def window(b):
        return slice(ROW - b, ROW - b + 8)

    def arrive(parity, q, s):
        a, b, c = VELOCITY[q]
        rows = window(b)
        amount = 32 * a + c
        if s < 4:
            base = turn(post[parity, q, slot_of(a, s - a), rows], amount)
            if c:
                halo = hro if 0 <= s - a < PLANES else hrx
                spot = center(s) if c == 1 else (center(s) - 1) % 128
                base = jnp.where(lane == spot, halo[q], base)
            return base
        base = post[parity, q, H_SLOT, rows]
        if a:
            outer = center(-1) if a == 1 else center(4)
            base = jnp.where((lane - outer + 16) % 128 < 32, post[parity, q, XH_SLOT, rows], base)
        if c:
            for p in range(4):
                spot = (center(p - a) - 1) % 128 if c == 1 else center(p - a)
                base = jnp.where(lane == spot, post[parity, q, slot_of(a, p - a), rows], base)
        return turn(base, amount)

    def flow_arrival(parity, s, key):
        q = FLOW_AT[key]
        if key == (0, 0, 0):
            return post[parity, q, own_slot(q, s), ROW : ROW + 8]
        back = FLOW_AT[tuple(-v for v in key)]
        value = arrive(parity, q, s)
        return jnp.where(value != value, post[parity, back, own_slot(back, s), ROW : ROW + 8], value)

    def needs_edge(s, key):
        a, b, c = key
        return a != 0 and b != 0 and (s == 4 or (s == 0 and a == 1) or (s == 3 and a == -1))

    def halo_rolls(parity, kind):
        for q in range(27):
            a, b, c = VELOCITY[q]
            if c and kind == "own":
                hro[q] = turn(post[parity, q, H_SLOT, window(b)], 32 * a + c)
            elif c and a and kind == ("edge" if b else "face"):
                hrx[q] = turn(post[parity, q, XH_SLOT, window(b)], 32 * a + c)

    def start_flow(parity, s, f, g, turned):
        old = aux[0, s]
        heat = old if turned is None else jnp.where(turned, sum_heat(g), old)
        flow, (inverse, jx, jy, jz) = collide_flow(f, heat, coef)
        if turned is not None:
            jz = jz + (0.5 * BUOYANCY) * (old - REFERENCE_HEAT)
            fresh = [j * inverse for j in (jx, jy, jz)]
            fresh = [jnp.where(v == v, v, 0.0) for v in fresh]
            aux[0, s] = heat
            for n in range(3):
                aux[1 + n, s] = jnp.where(turned, fresh[n], aux[1 + n, s])
        put(parity, s, {FLOW_AT[key]: flow[key] for key in FLOW})

    def start_heat(parity, s, g):
        out = collide_heat(g, [aux[1 + n, s] for n in range(3)], aux[4, s])
        put(parity, s, {HEAT_AT[k]: out[k] for k in range(7)})

    def staged(s, keys):
        return {key: stage[FLOW_AT[key], s] for key in keys}

    def staged_heat(s):
        return [stage[HEAT_AT[k], s] for k in range(7)]

    def heat_arrivals(parity):
        for k in (5, 6):
            q = HEAT_AT[k]
            hro[q] = turn(post[parity, q, H_SLOT, ROW : ROW + 8], VELOCITY[q][2])
        for s in range(5):
            for k in range(7):
                stage[HEAT_AT[k], s] = arrive(parity, HEAT_AT[k], s)

    def heat_collide(parity):
        for s in range(5):
            start_heat(parity, s, staged_heat(s))

    first = round_copies(0)
    for s in (4, 3, 0):
        start_flow(0, s, staged(s, FLOW), None, None)
        for copy in first[:2] if s == 0 else first[2:FIRST_X] if s == 3 else []:
            copy.start()
    for copy in late_copies:
        copy.start()
    for s in (1, 2):
        start_flow(0, s, staged(s, FLOW), None, None)
    for copy in first[FIRST_X:FIRST_HEAT]:
        copy.start()
    for copy in late_copies:
        copy.wait()
    for p in range(4):
        for k in range(7):
            stage[HEAT_AT[k], p] = turn(ar[p, k], center(p))
        aux[4, p] = omega_of(turn(ari[p], center(p)))
    heat_collide(0)
    for copy in first[FIRST_HEAT:]:
        copy.start()

    total = STEPS * WINDOWS

    def home_copy(src, dst, n, d, to):
        return pltpu.make_async_remote_copy(src_ref=src, dst_ref=dst, send_sem=t_send.at[n, d], recv_sem=t_recv.at[n, d], device_id=to, device_id_type=MESH)

    def moved(n, by):
        return lax.rem(me[n] + by, sizes[n])

    def home_copies():
        out = []
        for d in (2, 3, 1, 0):
            j = lax.rem(mine + d, 4)
            up = moved("gx", jnp.where(j == 0, 1, 0))
            down = moved("gx", jnp.where(j == 3, sizes["gx"] - 1, 0))
            out.append((home_copy(gs.at[lax.rem(j + 3, 4), 5], own.at[mine, 5], 1, d, (j, up, me["gy"])), mine == 0 if d == 0 else None))
            out.append((home_copy(gs.at[lax.rem(j + 1, 4), 6], own.at[mine, 6], 2, d, (j, down, me["gy"])), mine == 3 if d == 0 else None))
            if d:
                out.append((home_copy(gs.at[j, 0:5], own.at[mine, 0:5], 0, d, (j, me["gx"], me["gy"])), None))
            out.append((home_copy(gs.at[j, 3, 7:8], own_row.at[mine, 0, 7:8], 3, d, (j, me["gx"], moved("gy", 1))), None))
            out.append((home_copy(gs.at[j, 4, 0:1], own_row.at[mine, 1, 0:1], 4, d, (j, me["gx"], moved("gy", sizes["gy"] - 1))), None))
        return out

    def perform(copies, what):
        for copy, only in copies:
            if only is None:
                what(copy)
            else:
                pl.when(only)(functools.partial(what, copy))

    def home_start(parity):
        for p in range(4):
            for n, k in enumerate(HOME_ORDER):
                q = HEAT_AT[k]
                gs[p, n] = turn(post[parity, q, own_slot(q, p), ROW : ROW + 8], -center(p))
        perform(home_copies(), lambda copy: copy.start())
        own[mine, 0:5] = gs[mine, 0:5]

        @pl.when(mine != 0)
        def _():
            own[mine, 5] = gs[lax.rem(mine + 3, 4), 5]

        @pl.when(mine != 3)
        def _():
            own[mine, 6] = gs[lax.rem(mine + 1, 4), 6]

    def advance(step, carry):
        before = lax.rem(step + 1, 2)
        after = lax.rem(step, 2)
        turned = jnp.broadcast_to(step == STEPS, (8, 128))
        copies = round_copies(before)
        later = round_copies(after)

        def receive_heat():
            for copy in copies[FIRST_HEAT:]:
                copy.wait()
            heat_arrivals(before)

        def send_heat():
            heat_collide(after)
            for copy in later[FIRST_HEAT:]:
                copy.start()

        @pl.when(step == STEPS)
        def _():
            receive_heat()

        @pl.when(step > STEPS)
        def _():
            receive_heat()

            @pl.when(step < total - 1)
            def _():
                send_heat()

            @pl.when(step == total - 1)
            def _():
                heat_collide(after)
                home_start(after)

        for copy in copies[FIRST_Y:FIRST_HEAT]:
            copy.wait()
        halo_rolls(before, "own")
        for s in (1, 2):
            start_flow(after, s, {key: flow_arrival(before, s, key) for key in FLOW}, staged_heat(s), turned)
        for copy in copies[FIRST_X:FIRST_Y]:
            copy.wait()
        halo_rolls(before, "face")
        for s in (4, 0, 3):
            for key in FLOW:
                if not needs_edge(s, key):
                    stage[FLOW_AT[key], s] = flow_arrival(before, s, key)
        for copy in copies[:FIRST_X]:
            copy.wait()
        halo_rolls(before, "edge")
        for s in (4, 3, 0):
            f = {key: flow_arrival(before, s, key) if needs_edge(s, key) else stage[FLOW_AT[key], s] for key in FLOW}
            start_flow(after, s, f, staged_heat(s), turned)
            if s == 0:
                for copy in later[:2] + later[FIRST_X + 1 : FIRST_Y]:
                    copy.start()
            if s == 3:
                for copy in later[2:FIRST_X] + later[FIRST_X : FIRST_X + 1]:
                    copy.start()
        for copy in later[FIRST_Y:FIRST_HEAT]:
            copy.start()

        @pl.when(step < STEPS)
        def _():
            receive_heat()
            send_heat()

        @pl.when(step == STEPS)
        def _():
            send_heat()

        return carry

    lax.fori_loop(1, total, advance, 0)

    last = (total - 1) % 2
    copies = round_copies(last)

    def finish(p, edge):
        for n, key in enumerate(FLOW):
            if needs_edge(p, key) == edge:
                fout[n, p] = jnp.where(solid_ref[p] != 0, pop_ref[n, p], turn(flow_arrival(last, p, key), -center(p)))

    for copy in copies[FIRST_Y:FIRST_HEAT]:
        copy.wait()
    halo_rolls(last, "own")
    for p in (1, 2):
        finish(p, False)
    for copy in copies[FIRST_X:FIRST_Y]:
        copy.wait()
    halo_rolls(last, "face")
    for p in (0, 3):
        finish(p, False)
    for copy in copies[:FIRST_X]:
        copy.wait()
    halo_rolls(last, "edge")
    for p in (0, 3):
        finish(p, True)
    perform(home_copies(), lambda copy: copy.wait())
    row = lax.broadcasted_iota(jnp.int32, (8, 128), 0)
    for n in range(4):
        tiles = {k: own[n, place] for place, k in enumerate(HOME_ORDER)}
        tiles[3] = pltpu.roll(jnp.where(row == 7, own_row[n, 0], tiles[3]), 1, 0)
        tiles[4] = pltpu.roll(jnp.where(row == 0, own_row[n, 1], tiles[4]), 7, 0)
        tiles[5] = turn(jnp.where(lane == 127, own[(n + 3) % 4, HOME_ORDER.index(5)], tiles[5]), 1)
        tiles[6] = turn(jnp.where(lane == 0, own[(n + 1) % 4, HOME_ORDER.index(6)], tiles[6]), -1)
        for k in range(7):
            tout[k, 0, :, 128 * n : 128 * n + 128] = tiles[k]


def write_out(flow, heat, fout, tout, sem):
    copies = [pltpu.make_async_copy(src, dst, sem.at[n]) for n, (src, dst) in enumerate(((flow, fout), (heat, tout)))]
    for copy in copies:
        copy.start()
    for copy in copies:
        copy.wait()


def solution(mesh):
    sizes = dict(mesh.shape)

    def on_device(populations, thermal, velocity_prev, solid, phase_ids, conductivity, rates):
        vmem = pl.BlockSpec(memory_space=pltpu.VMEM)
        hbm = pl.BlockSpec(memory_space=pltpu.HBM)
        tile = (8, 128)
        flow, heat = pl.pallas_call(
            functools.partial(kernel, sizes),
            out_shape=(jax.ShapeDtypeStruct(populations.shape, F32), jax.ShapeDtypeStruct(thermal.shape, F32)),
            in_specs=[hbm] * 7,
            out_specs=(vmem, vmem),
            scratch_shapes=[pltpu.VMEM(v.shape, v.dtype) for v in (populations, thermal, velocity_prev, solid, phase_ids)]
            + [pltpu.SMEM(v.shape, v.dtype) for v in (conductivity, rates)]
            + [
                pltpu.VMEM((2, COUNT, 7, 24, 128), F32),
                pltpu.VMEM((COUNT, 5) + tile, F32),
                pltpu.VMEM((5, 5) + tile, F32),
                pltpu.VMEM((len(COEF),) + tile, F32),
                pltpu.VMEM((COUNT,) + tile, F32),
                pltpu.VMEM((COUNT,) + tile, F32),
                pltpu.VMEM((4, 7) + tile, F32),
                pltpu.VMEM((4,) + tile, jnp.int32),
                pltpu.VMEM((4, 2) + tile, F32),
                pltpu.VMEM((4, 2) + tile, F32),
                pltpu.VMEM((2, 8) + tile, F32),
                pltpu.VMEM((2, 8) + tile, F32),
                pltpu.VMEM((4, 7) + tile, F32),
                pltpu.VMEM((4, 7) + tile, F32),
                pltpu.VMEM((4, 2) + tile, F32),
                pltpu.SemaphoreType.DMA((7,)),
                pltpu.SemaphoreType.DMA((2, len(MESSAGES))),
                pltpu.SemaphoreType.DMA((2, len(MESSAGES))),
                pltpu.SemaphoreType.DMA((3, 3)),
                pltpu.SemaphoreType.DMA((3, 3)),
                pltpu.SemaphoreType.DMA((2,)),
                pltpu.SemaphoreType.DMA((2,)),
                pltpu.SemaphoreType.DMA((5, 4)),
                pltpu.SemaphoreType.DMA((5, 4)),
            ],
            compiler_params=pltpu.CompilerParams(collective_id=0, has_side_effects=True, vmem_limit_bytes=48 * 1024 * 1024),
        )(*[pltpu.with_memory_space_constraint(v, pltpu.HBM) for v in (populations, thermal, velocity_prev, solid, phase_ids, conductivity, rates)])
        anywhere = pl.BlockSpec(memory_space=pl.ANY)
        return pl.pallas_call(
            write_out,
            out_shape=(jax.ShapeDtypeStruct(flow.shape, F32), jax.ShapeDtypeStruct(heat.shape, F32)),
            in_specs=[anywhere] * 2,
            out_specs=(anywhere, anywhere),
            scratch_shapes=[pltpu.SemaphoreType.DMA((2,))],
            compiler_params=pltpu.CompilerParams(vmem_limit_bytes=4 * 1024 * 1024),
        )(flow, heat)

    in_specs = (
        P(None, "gx", "gy", "grp"),
        P(None, ("gx", "grp"), "gy", None),
        P(None, "gx", "gy", "grp"),
        P("gx", "gy", "grp"),
        P(("gx", "grp"), "gy", None),
        P(),
        P(),
    )
    out_specs = (P(None, "gx", "gy", "grp"), P(None, ("gx", "grp"), "gy", None))
    return jax.shard_map(on_device, mesh=mesh, in_specs=in_specs, out_specs=out_specs, check_vma=False)
```

```python
import functools

import jax
import jax.numpy as jnp
import numpy as np
from jax import lax
from jax.experimental import pallas as pl
from jax.experimental.pallas import tpu as pltpu
from jax.sharding import PartitionSpec as P

STEPS = 4
WINDOWS = 2
BUOYANCY = 0.03
REFERENCE_HEAT = 1.0
MESH = pl.DeviceIdType.MESH
F32 = jnp.float32

RING = [(-1, -1), (-1, 0), (-1, 1), (0, 1), (1, 1), (1, 0), (1, -1), (0, -1), (0, 0), "0", "x+", "x-", "y+", "y-", "z+", "z-"]
THERMAL = {"0": (0, 0, 0), "x+": (1, 0, 0), "x-": (-1, 0, 0), "y+": (0, 1, 0), "y-": (0, -1, 0), "z+": (0, 0, 1), "z-": (0, 0, -1)}
HOME_ORDER = [0, 5, 6, 3, 4, 1, 2]
HEAT_ORDER = ["0", "x+", "x-", "y+", "y-", "z+", "z-"]
VELOCITY = []
FLOW_AT = {}
HEAT_AT = {}
for entry in RING:
    if isinstance(entry, str):
        HEAT_AT[HEAT_ORDER.index(entry)] = len(VELOCITY)
        VELOCITY.append(THERMAL[entry])
    else:
        for c in (-1, 0, 1):
            FLOW_AT[entry + (c,)] = len(VELOCITY)
            VELOCITY.append(entry + (c,))
COUNT = len(VELOCITY)
FLOW = [(a, b, c) for a in (-1, 0, 1) for b in (-1, 0, 1) for c in (-1, 0, 1)]
X_GROUP = {-1: (0, 9), 1: (12, 21)}
Y_GROUP = {1: [(6, 15)], -1: [(18, 24), (0, 3)]}
EDGE_GROUP = {(-1, -1): (0, 3), (-1, 1): (6, 9), (1, 1): (12, 15), (1, -1): (18, 21)}
X_SLOT, XH_SLOT, H_SLOT = 0, 1, 6
PLANES = 4
ROW = 8
SOURCE_ROW = {1: (15, 7), -1: (8, 16)}


def center(plane):
    return 32 * (plane + 1) % 128


def slot_of(a, plane):
    if plane < 0 or plane >= PLANES:
        return X_SLOT
    return 2 + (plane if a >= 0 else PLANES - 1 - plane)


def turn(value, amount):
    amount = amount % 128
    return pltpu.roll(value, amount, 1) if amount else value


MESSAGES = []
for (a, b), span in EDGE_GROUP.items():
    s, t = SOURCE_ROW[b]
    MESSAGES.append(((0, a, b), span, (5, 7), (0, 2), (s, s + 1), (t, t + 1)))
FIRST_X = len(MESSAGES)
for a in (1, -1):
    MESSAGES.append(((0, a, 0), X_GROUP[a], (5, 7), (0, 2), (ROW, ROW + 8), (ROW, ROW + 8)))
FIRST_Y = len(MESSAGES)
for b in (1, -1):
    s, t = SOURCE_ROW[b]
    for span in Y_GROUP[b]:
        MESSAGES.append(((0, 0, b), span, (2, 7), (2, 7), (s, s + 1), (t, t + 1)))

FIRST_HEAT = len(MESSAGES)
for a in (1, -1):
    q = HEAT_AT[HEAT_ORDER.index("x+" if a == 1 else "x-")]
    MESSAGES.append(((0, a, 0), (q, q + 1), (5, 7), (0, 2), (ROW, ROW + 8), (ROW, ROW + 8)))
for b in (1, -1):
    q = HEAT_AT[HEAT_ORDER.index("y+" if b == 1 else "y-")]
    s, t = SOURCE_ROW[b]
    MESSAGES.append(((0, 0, b), (q, q + 1), (2, 7), (2, 7), (s, s + 1), (t, t + 1)))

RELAXED = [m for m in [(p, q, r) for p in range(3) for q in range(3) for r in range(3)] if m not in ((0, 0, 0), (0, 0, 1), (0, 1, 0), (1, 0, 0))]
COEF = {}
for m in RELAXED:
    COEF[m, "keep"] = len(COEF)
    if m != (1, 1, 1):
        COEF[m, "gain"] = len(COEF)


def gain_scale(m):
    odd = sum(v == 1 for v in m)
    two = sum(v == 2 for v in m)
    return 3.0 ** (-(max(two - 1, 0) if odd == 0 else two))


def collide_flow(f, heat, coef):
    for axis in range(3):
        g = {}
        for one in (-1, 0, 1):
            for two in (-1, 0, 1):
                def at(v):
                    key = [one, two]
                    key.insert(axis, v)
                    return tuple(key)
                low, mid, high = f[at(-1)], f[at(0)], f[at(1)]
                both = high + low
                g[at(-1)] = both + mid
                g[at(0)] = high - low
                g[at(1)] = both
        f = g
    m = {(p, q, r): f[p - 1, q - 1, r - 1] for p in range(3) for q in range(3) for r in range(3)}
    rho, jx, jy, jz = m[0, 0, 0], m[1, 0, 0], m[0, 1, 0], m[0, 0, 1]
    force = BUOYANCY * (heat - REFERENCE_HEAT)
    flow_z = jz + 0.5 * force
    inverse = 1.0 / rho
    ux, uy, uz = jx * inverse, jy * inverse, flow_z * inverse
    third = rho * (1.0 / 3.0)
    xx, yy, zz = jx * ux, jy * uy, flow_z * uz
    square = {0: xx, 1: yy, 2: zz}
    flux = {0: jx, 1: jy, 2: flow_z}
    cross = {(0, 1): jx * uy, (0, 2): jx * uz, (1, 2): jy * uz}
    out = {}
    for k in RELAXED:
        odd = tuple(n for n in range(3) if k[n] == 1)
        if len(odd) == 3:
            out[k] = m[k] * coef(k, "keep")
            continue
        if len(odd) == 0:
            base = third
            for n in range(3):
                if k[n] == 2:
                    base = base + square[n]
        elif len(odd) == 1:
            base = flux[odd[0]]
        else:
            base = cross[odd]
        out[k] = m[k] * coef(k, "keep") + base * coef(k, "gain")
    out[0, 0, 0] = rho
    out[1, 0, 0] = 0.5 * jx
    out[0, 1, 0] = 0.5 * jy
    out[0, 0, 1] = 0.5 * (jz + force)
    f = {tuple(v - 1 for v in k): out[k] for k in out}
    for axis in range(3):
        g = {}
        for one in (-1, 0, 1):
            for two in (-1, 0, 1):
                def at(v):
                    key = [one, two]
                    key.insert(axis, v)
                    return tuple(key)
                zero, first, second = f[at(-1)], f[at(0)], f[at(1)]
                half = 0.5 * second
                g[at(-1)] = half - first
                g[at(0)] = zero - second
                g[at(1)] = half + first
        f = g
    return f, (inverse, jx, jy, jz)


def collide_heat(g, speed, omega):
    total = g[0]
    for k in range(1, 7):
        total = total + g[k]
    keep = 1.0 - omega
    part = omega * total * 0.125
    four = 4.0 * part
    out = [keep * g[0] + 2.0 * part]
    for d in range(3):
        push = four * speed[d]
        out.append(keep * g[1 + 2 * d] + (part + push))
        out.append(keep * g[2 + 2 * d] + (part - push))
    return out


def sum_heat(g):
    total = g[0]
    for k in range(1, 7):
        total = total + g[k]
    return total


def kernel(sizes, pop_in, th_in, vel_in, solid_in, ph_in, cond_in, rates_in, fout, tout, pop_ref, th_ref, vel_ref, solid_ref, ph_ref, cond_ref, rates_ref,
           post, stage, aux, coefs, hro, hrx, ar, ari, aps, apr, zs, zr, gs, own, own_row,
           in_sem, send_sem, recv_sem, a_send, a_recv, z_send, z_recv, t_send, t_recv):
    loads = [pltpu.make_async_copy(src, dst, in_sem.at[n]) for n, (src, dst) in enumerate((
        (th_in, th_ref), (ph_in, ph_ref), (pop_in, pop_ref), (solid_in, solid_ref), (vel_in, vel_ref), (rates_in, rates_ref), (cond_in, cond_ref)))]
    for copy in loads:
        copy.start()
    me = {n: lax.axis_index(n) for n in sizes}
    names = list(sizes)

    def device(offset):
        return tuple(lax.rem(me[n] + (k + sizes[n]), sizes[n]) if k else me[n] for n, k in zip(names, offset))

    mine = me["grp"]
    barrier = pltpu.get_barrier_semaphore()
    others = [(0, a, b) for a in (-1, 0, 1) for b in (-1, 0, 1) if (a, b) != (0, 0)] + [(d, 0, 0) for d in (1, 2, 3)]
    for offset in others:
        pl.semaphore_signal(barrier, inc=1, device_id=device(offset), device_id_type=MESH)

    lane = lax.broadcasted_iota(jnp.int32, (8, 128), 1)
    unit = (lane + 16) % 32

    def chunk(j):
        return pl.ds(pl.multiple_of(j * 128, 128), 128)

    loads[0].wait()
    loads[1].wait()
    for m in range(4):
        left, right = slice(128 * ((m + 3) % 4), 128 * ((m + 3) % 4) + 128), slice(128 * ((m + 1) % 4), 128 * ((m + 1) % 4) + 128)
        pack = None
        for k in range(8):
            if k < 7:
                both = jnp.where(lane < 64, th_ref[k, 0, :, right], th_ref[k, 0, :, left])
            else:
                both = jnp.where(lane < 64, ph_ref[0, :, right], ph_ref[0, :, left]).astype(F32)
            both = turn(both, 16 * k + 8)
            pack = both if pack is None else jnp.where(lane // 16 == k, both, pack)
        aps[m, 0] = pack
        aps[m, 1] = sum_heat([th_ref[k, 0, :, 128 * m : 128 * m + 128] for k in range(7)])
    apr[mine] = aps[mine]
    ar[mine] = th_ref[:, 0, :, chunk(mine)]
    ari[mine] = ph_ref[0, :, chunk(mine)]

    group = [(unit == unit) & (((lane - center(p) + 16) % 128) < 32) for p in range(4)]
    for copy in loads[2:5]:
        copy.wait()
    solid = [turn(solid_ref[p], center(p)) != 0 for p in range(4)]
    fields = [("f", key) for key in FLOW] + [("u", n) for n in range(3)]

    def merged(field):
        kind, key = field
        tile = None
        for p in range(4):
            if kind == "f":
                value = turn(pop_ref[FLOW.index(key), p], center(p))
                value = jnp.where(solid[p], jnp.nan, value)
                stage[FLOW_AT[key], p] = value
            else:
                value = turn(vel_ref[key, p], center(p))
                aux[1 + key, p] = value
            tile = value if tile is None else jnp.where(group[p], value, tile)
        return tile

    for n in range(8):
        low, high = None, None
        for k, field in enumerate(fields[4 * n : 4 * n + 4]):
            value = turn(merged(field), 8 * k - 8)
            low = value if low is None else jnp.where(unit // 8 == k, value, low)
            high = value if high is None else jnp.where(unit // 8 == (k + 1) % 4, value, high)
        zs[0, n] = low
        zs[1, n] = high

    loads[5].wait()
    loads[6].wait()
    for k in RELAXED:
        rate = rates_ref[9 * k[0] + 3 * k[1] + k[2]]
        half = 0.5 ** sum(v == 1 for v in k)
        coefs[COEF[k, "keep"]] = jnp.full((8, 128), (1.0 - rate) * half, F32)
        if (k, "gain") in COEF:
            coefs[COEF[k, "gain"]] = jnp.full((8, 128), rate * (half * gain_scale(k)), F32)

    def coef(k, kind):
        return coefs[COEF[k, kind]]

    pl.semaphore_wait(barrier, len(others))
    first_copies, late_copies = [], []
    for d in (2, 1, 3):
        target = lax.rem(mine + d, 4)
        for n, (src, dst) in enumerate(((aps.at[target], apr.at[mine]), (th_ref.at[:, 0, :, chunk(target)], ar.at[mine]), (ph_ref.at[0, :, chunk(target)], ari.at[mine]))):
            copy = pltpu.make_async_remote_copy(src_ref=src, dst_ref=dst, send_sem=a_send.at[n, d - 1], recv_sem=a_recv.at[n, d - 1], device_id=device((d, 0, 0)), device_id_type=MESH)
            (late_copies if n else first_copies).append(copy)
    z_copies = [pltpu.make_async_remote_copy(src_ref=zs.at[side], dst_ref=zr.at[side], send_sem=z_send.at[side], recv_sem=z_recv.at[side], device_id=device((d, 0, 0)), device_id_type=MESH) for side, d in ((0, 1), (1, -1))]
    for copy in first_copies + z_copies:
        copy.start()

    def omega_of(ids):
        level = jnp.full((8, 128), cond_ref[3], F32)
        for n in range(3):
            level = jnp.where(ids == n, cond_ref[n], level)
        return 1.0 / (0.5 + 4.0 * level)

    for copy in first_copies:
        copy.wait()
    for p in range(4):
        aux[0, p] = turn(apr[p, 1], center(p))
    tiles = []
    for k in range(8):
        tile = None
        for p in range(4):
            value = turn(apr[p, 0], center(p) - 16 * k - 8)
            tile = value if tile is None else jnp.where(group[p], value, tile)
        tiles.append(tile)
    for k in range(7):
        stage[HEAT_AT[k], 4] = tiles[k]
    aux[0, 4] = sum_heat(tiles[:7])
    aux[4, 4] = omega_of(tiles[7])

    for copy in z_copies:
        copy.wait()
    for n in range(8):
        low, high = zr[0, n], zr[1, n]
        for k, (kind, key) in enumerate(fields[4 * n : 4 * n + 4]):
            value = turn(jnp.where(unit // 8 == k, low, high), 8 - 8 * k)
            if kind == "f":
                stage[FLOW_AT[key], 4] = value
            else:
                aux[1 + key, 4] = value

    def round_copies(parity):
        out = []
        for n, (offset, span, s_slots, t_slots, s_rows, t_rows) in enumerate(MESSAGES):
            out.append(pltpu.make_async_remote_copy(
                src_ref=post.at[parity, span[0] : span[1], s_slots[0] : s_slots[1], s_rows[0] : s_rows[1]],
                dst_ref=post.at[parity, span[0] : span[1], t_slots[0] : t_slots[1], t_rows[0] : t_rows[1]],
                send_sem=send_sem.at[parity, n], recv_sem=recv_sem.at[parity, n], device_id=device(offset), device_id_type=MESH))
        return out

    def own_slot(q, s):
        return H_SLOT if s == 4 else slot_of(VELOCITY[q][0], s)

    def put(parity, s, tiles):
        for q, value in tiles.items():
            post[parity, q, own_slot(q, s), ROW : ROW + 8] = value

    def window(b):
        return slice(ROW - b, ROW - b + 8)

    def arrive(parity, q, s):
        a, b, c = VELOCITY[q]
        rows = window(b)
        amount = 32 * a + c
        if s < 4:
            base = turn(post[parity, q, slot_of(a, s - a), rows], amount)
            if c:
                halo = hro if 0 <= s - a < PLANES else hrx
                spot = center(s) if c == 1 else (center(s) - 1) % 128
                base = jnp.where(lane == spot, halo[q], base)
            return base
        base = post[parity, q, H_SLOT, rows]
        if a:
            outer = center(-1) if a == 1 else center(4)
            base = jnp.where((lane - outer + 16) % 128 < 32, post[parity, q, XH_SLOT, rows], base)
        if c:
            for p in range(4):
                spot = (center(p - a) - 1) % 128 if c == 1 else center(p - a)
                base = jnp.where(lane == spot, post[parity, q, slot_of(a, p - a), rows], base)
        return turn(base, amount)

    def flow_arrival(parity, s, key):
        q = FLOW_AT[key]
        if key == (0, 0, 0):
            return post[parity, q, own_slot(q, s), ROW : ROW + 8]
        back = FLOW_AT[tuple(-v for v in key)]
        value = arrive(parity, q, s)
        return jnp.where(value != value, post[parity, back, own_slot(back, s), ROW : ROW + 8], value)

    def needs_edge(s, key):
        a, b, c = key
        return a != 0 and b != 0 and (s == 4 or (s == 0 and a == 1) or (s == 3 and a == -1))

    def halo_rolls(parity, kind):
        for q in range(27):
            a, b, c = VELOCITY[q]
            if c and kind == ("own" if b else "still"):
                hro[q] = turn(post[parity, q, H_SLOT, window(b)], 32 * a + c)
            elif c and a and kind == ("edge" if b else "face"):
                hrx[q] = turn(post[parity, q, XH_SLOT, window(b)], 32 * a + c)

    def start_flow(parity, s, f, g, turned):
        old = aux[0, s]
        heat = old if turned is None else jnp.where(turned, sum_heat(g), old)
        flow, (inverse, jx, jy, jz) = collide_flow(f, heat, coef)
        if turned is not None:
            jz = jz + (0.5 * BUOYANCY) * (old - REFERENCE_HEAT)
            fresh = [j * inverse for j in (jx, jy, jz)]
            fresh = [jnp.where(v == v, v, 0.0) for v in fresh]
            aux[0, s] = heat
            for n in range(3):
                aux[1 + n, s] = jnp.where(turned, fresh[n], aux[1 + n, s])
        put(parity, s, {FLOW_AT[key]: flow[key] for key in FLOW})

    def start_heat(parity, s, g):
        out = collide_heat(g, [aux[1 + n, s] for n in range(3)], aux[4, s])
        put(parity, s, {HEAT_AT[k]: out[k] for k in range(7)})

    def staged(s, keys):
        return {key: stage[FLOW_AT[key], s] for key in keys}

    def staged_heat(s):
        return [stage[HEAT_AT[k], s] for k in range(7)]

    def heat_arrivals(parity):
        for k in (5, 6):
            q = HEAT_AT[k]
            hro[q] = turn(post[parity, q, H_SLOT, ROW : ROW + 8], VELOCITY[q][2])
        for s in range(5):
            for k in range(7):
                stage[HEAT_AT[k], s] = arrive(parity, HEAT_AT[k], s)

    def heat_collide(parity):
        for s in range(5):
            start_heat(parity, s, staged_heat(s))

    first = round_copies(0)
    for s in (4, 3, 0):
        start_flow(0, s, staged(s, FLOW), None, None)
        for copy in first[:2] if s == 0 else first[2:FIRST_X] if s == 3 else []:
            copy.start()
    for copy in late_copies:
        copy.start()
    for s in (1, 2):
        start_flow(0, s, staged(s, FLOW), None, None)
    for copy in first[FIRST_X:FIRST_HEAT]:
        copy.start()
    for copy in late_copies:
        copy.wait()
    for p in range(4):
        for k in range(7):
            stage[HEAT_AT[k], p] = turn(ar[p, k], center(p))
        aux[4, p] = omega_of(turn(ari[p], center(p)))
    heat_collide(0)
    for copy in first[FIRST_HEAT:]:
        copy.start()

    total = STEPS * WINDOWS

    def home_copy(src, dst, n, d, to):
        return pltpu.make_async_remote_copy(src_ref=src, dst_ref=dst, send_sem=t_send.at[n, d], recv_sem=t_recv.at[n, d], device_id=to, device_id_type=MESH)

    def moved(n, by):
        return lax.rem(me[n] + by, sizes[n])

    def home_copies():
        out = []
        for d in (2, 3, 1, 0):
            j = lax.rem(mine + d, 4)
            up = moved("gx", jnp.where(j == 0, 1, 0))
            down = moved("gx", jnp.where(j == 3, sizes["gx"] - 1, 0))
            out.append((home_copy(gs.at[lax.rem(j + 3, 4), 5], own.at[mine, 5], 1, d, (j, up, me["gy"])), mine == 0 if d == 0 else None))
            out.append((home_copy(gs.at[lax.rem(j + 1, 4), 6], own.at[mine, 6], 2, d, (j, down, me["gy"])), mine == 3 if d == 0 else None))
            if d:
                out.append((home_copy(gs.at[j, 0:5], own.at[mine, 0:5], 0, d, (j, me["gx"], me["gy"])), None))
            out.append((home_copy(gs.at[j, 3, 7:8], own_row.at[mine, 0, 7:8], 3, d, (j, me["gx"], moved("gy", 1))), None))
            out.append((home_copy(gs.at[j, 4, 0:1], own_row.at[mine, 1, 0:1], 4, d, (j, me["gx"], moved("gy", sizes["gy"] - 1))), None))
        return out

    def perform(copies, what):
        for copy, only in copies:
            if only is None:
                what(copy)
            else:
                pl.when(only)(functools.partial(what, copy))

    def home_start(parity):
        for p in range(4):
            for n, k in enumerate(HOME_ORDER):
                q = HEAT_AT[k]
                gs[p, n] = turn(post[parity, q, own_slot(q, p), ROW : ROW + 8], -center(p))
        perform(home_copies(), lambda copy: copy.start())
        own[mine, 0:5] = gs[mine, 0:5]

        @pl.when(mine != 0)
        def _():
            own[mine, 5] = gs[lax.rem(mine + 3, 4), 5]

        @pl.when(mine != 3)
        def _():
            own[mine, 6] = gs[lax.rem(mine + 1, 4), 6]

    def advance(step, carry):
        before = lax.rem(step + 1, 2)
        after = lax.rem(step, 2)
        turned = jnp.broadcast_to(step == STEPS, (8, 128))
        copies = round_copies(before)
        later = round_copies(after)

        def receive_heat():
            for copy in copies[FIRST_HEAT:]:
                copy.wait()
            heat_arrivals(before)

        def send_heat():
            heat_collide(after)
            for copy in later[FIRST_HEAT:]:
                copy.start()

        @pl.when(step == STEPS)
        def _():
            receive_heat()

        @pl.when(step > STEPS)
        def _():
            receive_heat()

            @pl.when(step < total - 1)
            def _():
                send_heat()

            @pl.when(step == total - 1)
            def _():
                heat_collide(after)
                home_start(after)

        halo_rolls(before, "still")
        for s in (1, 2):
            for key in FLOW:
                if key[1] == 0:
                    stage[FLOW_AT[key], s] = flow_arrival(before, s, key)
        for copy in copies[FIRST_Y:FIRST_HEAT]:
            copy.wait()
        halo_rolls(before, "own")
        for s in (1, 2):
            f = {key: flow_arrival(before, s, key) if key[1] else stage[FLOW_AT[key], s] for key in FLOW}
            start_flow(after, s, f, staged_heat(s), turned)
        for copy in copies[FIRST_X:FIRST_Y]:
            copy.wait()
        halo_rolls(before, "face")
        for s in (4, 0, 3):
            for key in FLOW:
                if not needs_edge(s, key):
                    stage[FLOW_AT[key], s] = flow_arrival(before, s, key)
        for copy in copies[:FIRST_X]:
            copy.wait()
        halo_rolls(before, "edge")
        for s in (4, 3, 0):
            f = {key: flow_arrival(before, s, key) if needs_edge(s, key) else stage[FLOW_AT[key], s] for key in FLOW}
            start_flow(after, s, f, staged_heat(s), turned)
            if s == 0:
                for copy in later[:2] + later[FIRST_X + 1 : FIRST_Y]:
                    copy.start()
            if s == 3:
                for copy in later[2:FIRST_X] + later[FIRST_X : FIRST_X + 1]:
                    copy.start()
        for copy in later[FIRST_Y:FIRST_HEAT]:
            copy.start()

        @pl.when(step < STEPS)
        def _():
            receive_heat()
            send_heat()

        @pl.when(step == STEPS)
        def _():
            send_heat()

        return carry

    lax.fori_loop(1, total, advance, 0)

    last = (total - 1) % 2
    copies = round_copies(last)

    def finish(p, edge):
        for n, key in enumerate(FLOW):
            if needs_edge(p, key) == edge:
                fout[n, p] = jnp.where(solid_ref[p] != 0, pop_ref[n, p], turn(flow_arrival(last, p, key), -center(p)))

    for copy in copies[FIRST_Y:FIRST_HEAT]:
        copy.wait()
    halo_rolls(last, "still")
    halo_rolls(last, "own")
    for p in (1, 2):
        finish(p, False)
    for copy in copies[FIRST_X:FIRST_Y]:
        copy.wait()
    halo_rolls(last, "face")
    for p in (0, 3):
        finish(p, False)
    for copy in copies[:FIRST_X]:
        copy.wait()
    halo_rolls(last, "edge")
    for p in (0, 3):
        finish(p, True)
    perform(home_copies(), lambda copy: copy.wait())
    row = lax.broadcasted_iota(jnp.int32, (8, 128), 0)
    for n in range(4):
        tiles = {k: own[n, place] for place, k in enumerate(HOME_ORDER)}
        tiles[3] = pltpu.roll(jnp.where(row == 7, own_row[n, 0], tiles[3]), 1, 0)
        tiles[4] = pltpu.roll(jnp.where(row == 0, own_row[n, 1], tiles[4]), 7, 0)
        tiles[5] = turn(jnp.where(lane == 127, own[(n + 3) % 4, HOME_ORDER.index(5)], tiles[5]), 1)
        tiles[6] = turn(jnp.where(lane == 0, own[(n + 1) % 4, HOME_ORDER.index(6)], tiles[6]), -1)
        for k in range(7):
            tout[k, 0, :, 128 * n : 128 * n + 128] = tiles[k]


def write_out(flow, heat, fout, tout, sem):
    copies = [pltpu.make_async_copy(src, dst, sem.at[n]) for n, (src, dst) in enumerate(((flow, fout), (heat, tout)))]
    for copy in copies:
        copy.start()
    for copy in copies:
        copy.wait()


def solution(mesh):
    sizes = dict(mesh.shape)

    def on_device(populations, thermal, velocity_prev, solid, phase_ids, conductivity, rates):
        vmem = pl.BlockSpec(memory_space=pltpu.VMEM)
        hbm = pl.BlockSpec(memory_space=pltpu.HBM)
        tile = (8, 128)
        flow, heat = pl.pallas_call(
            functools.partial(kernel, sizes),
            out_shape=(jax.ShapeDtypeStruct(populations.shape, F32), jax.ShapeDtypeStruct(thermal.shape, F32)),
            in_specs=[hbm] * 7,
            out_specs=(vmem, vmem),
            scratch_shapes=[pltpu.VMEM(v.shape, v.dtype) for v in (populations, thermal, velocity_prev, solid, phase_ids)]
            + [pltpu.SMEM(v.shape, v.dtype) for v in (conductivity, rates)]
            + [
                pltpu.VMEM((2, COUNT, 7, 24, 128), F32),
                pltpu.VMEM((COUNT, 5) + tile, F32),
                pltpu.VMEM((5, 5) + tile, F32),
                pltpu.VMEM((len(COEF),) + tile, F32),
                pltpu.VMEM((COUNT,) + tile, F32),
                pltpu.VMEM((COUNT,) + tile, F32),
                pltpu.VMEM((4, 7) + tile, F32),
                pltpu.VMEM((4,) + tile, jnp.int32),
                pltpu.VMEM((4, 2) + tile, F32),
                pltpu.VMEM((4, 2) + tile, F32),
                pltpu.VMEM((2, 8) + tile, F32),
                pltpu.VMEM((2, 8) + tile, F32),
                pltpu.VMEM((4, 7) + tile, F32),
                pltpu.VMEM((4, 7) + tile, F32),
                pltpu.VMEM((4, 2) + tile, F32),
                pltpu.SemaphoreType.DMA((7,)),
                pltpu.SemaphoreType.DMA((2, len(MESSAGES))),
                pltpu.SemaphoreType.DMA((2, len(MESSAGES))),
                pltpu.SemaphoreType.DMA((3, 3)),
                pltpu.SemaphoreType.DMA((3, 3)),
                pltpu.SemaphoreType.DMA((2,)),
                pltpu.SemaphoreType.DMA((2,)),
                pltpu.SemaphoreType.DMA((5, 4)),
                pltpu.SemaphoreType.DMA((5, 4)),
            ],
            compiler_params=pltpu.CompilerParams(collective_id=0, has_side_effects=True, vmem_limit_bytes=48 * 1024 * 1024),
        )(*[pltpu.with_memory_space_constraint(v, pltpu.HBM) for v in (populations, thermal, velocity_prev, solid, phase_ids, conductivity, rates)])
        anywhere = pl.BlockSpec(memory_space=pl.ANY)
        return pl.pallas_call(
            write_out,
            out_shape=(jax.ShapeDtypeStruct(flow.shape, F32), jax.ShapeDtypeStruct(heat.shape, F32)),
            in_specs=[anywhere] * 2,
            out_specs=(anywhere, anywhere),
            scratch_shapes=[pltpu.SemaphoreType.DMA((2,))],
            compiler_params=pltpu.CompilerParams(vmem_limit_bytes=4 * 1024 * 1024),
        )(flow, heat)

    in_specs = (
        P(None, "gx", "gy", "grp"),
        P(None, ("gx", "grp"), "gy", None),
        P(None, "gx", "gy", "grp"),
        P("gx", "gy", "grp"),
        P(("gx", "grp"), "gy", None),
        P(),
        P(),
    )
    out_specs = (P(None, "gx", "gy", "grp"), P(None, ("gx", "grp"), "gy", None))
    return jax.shard_map(on_device, mesh=mesh, in_specs=in_specs, out_specs=out_specs, check_vma=False)
```
